256 devices in a mesh: row: 32 (over z_hi, x, core), col: 8 (over z_lo, y).
Axes of the slice: x: 4, y: 4, z: 8 (z_hi: 4, z_lo: 2; z = z_hi * 2 + z_lo), core: 2. Of those that a mesh axis runs over, the one named last changes fastest.
Arguments:
- density_factor: bfloat16 [6144, 512], P('row', 'col'), may hold values from -0.25 to 0.25
- hole_factor: bfloat16 [6144, 512], P('row', 'col'), may hold values from -0.25 to 0.25
- ph_factor: bfloat16 [6144, 512], P('row', 'col'), may hold values from -0.25 to 0.25
- hamiltonian: bfloat16 [6144, 6144], P('row', 'col'), as said below
- multiplier_q: bfloat16 [6144, 6144], P('row', 'col'), as said below
- multiplier_g: bfloat16 [6144, 6144], P('row', 'col'), as said below
- ph_perm: int32 [6144], replicated, may hold values from 0 to 6143, as said below
- block_lengths: int32 [48], replicated, may hold values from 1 to 256, 6144 in all
Outputs:
- grad_density: float32 [6144, 512], P('row', 'col')
- grad_hole: float32 [6144, 512], P('row', 'col')
- grad_ph: float32 [6144, 512], P('row', 'col')
The draws below stay inside these ranges and needn't reach their ends.
Inputs may be any that keep to these rules, and one draw needn't show every extreme that they name: `ph_perm`: a permutation of the rows; each aligned block of 192 entries holds exactly 6 values from each aligned range of 192 rows. `block_lengths`: the lengths sum to 6144. `hamiltonian`: symmetric. `multiplier_q`: symmetric. `multiplier_g`: symmetric.
All inputs are finite; a program needn't handle non-finite values.
Results may differ from the reference program's by a relative error of at most 0.00035.
The reference program's roundings to bfloat16 on the way (of `density_ph`) count: a program that leaves them out, or rounds other values in their place, can miss the bound.
Values may be sent and summed in bfloat16 or wider, within the bound.
No kernel may reach another device: no remote copies, remote signals or barrier semaphores. Data moves between devices by JAX's collectives and lax.ppermute only.
A program may use at most 64 MiB of HBM per device.

```python
import math
import jax
import jax.numpy as jnp
import numpy as np

NP = 6144
RANK = 512
SEGS = 48
MOSTLEN = 256
PH_BLOCK = 192
SENDS = 6


def symmetric_matrix(key, salt):
    base = jax.random.fold_in(key, salt)
    entries = jax.random.normal(jax.random.fold_in(base, 1), (NP, NP), jnp.float32)
    return ((entries + entries.T) * (0.15 / math.sqrt(2.0))).astype(jnp.bfloat16)


def draw_hamiltonian(key, part):
    return symmetric_matrix(key, 11)


def draw_multiplier_q(key, part):
    return symmetric_matrix(key, 12)


def draw_multiplier_g(key, part):
    return symmetric_matrix(key, 13)


def shuffle_block(subkey):
    return jax.random.permutation(subkey, PH_BLOCK).astype(jnp.int32)


def draw_ph_perm(key, part):
    groups = NP // PH_BLOCK
    base = jax.random.fold_in(key, 31)
    first_keys = jax.random.split(jax.random.fold_in(base, 1), groups)
    inner = jax.vmap(shuffle_block)(first_keys)
    source_rows = jnp.arange(groups, dtype=jnp.int32)[:, None] * PH_BLOCK + inner
    grouped = source_rows.reshape(groups, groups, SENDS).transpose(1, 0, 2).reshape(groups, PH_BLOCK)
    second_keys = jax.random.split(jax.random.fold_in(base, 2), groups)
    order = jax.vmap(shuffle_block)(second_keys)
    mixed = jnp.take_along_axis(grouped, order, axis=1)
    return mixed.reshape(NP).astype(jnp.int32)


def shard_levels(key, extent, cuts, smallest, top_value):
    def one(position, parts):
        heights = jax.random.uniform(jax.random.fold_in(jax.random.fold_in(key, 6), position), (parts,), jnp.float32, smallest / len(cuts), top_value / len(cuts))
        return jnp.repeat(jnp.exp(heights), extent[position] // parts).reshape((-1,) + (1,) * (len(extent) - position - 1))

    factor_of = one(*cuts[0])
    for cut in cuts[1:]:
        factor_of = factor_of * one(*cut)
    return factor_of


def profile(count, total, reach, lean):
    portions = [(1 << 20) // math.isqrt(standing ** lean) + 1 for standing in range(2, count + 1)]
    spare, counts = total - reach - (count - 1), [1] * (count - 1)
    while spare > 0:
        movable = [i for i in range(count - 1) if counts[i] < reach]
        whole, budget = sum([portions[i] for i in movable]), spare
        for i in movable:
            addition = min(reach - counts[i], max(1, budget * portions[i] // whole), spare)
            counts[i] = counts[i] + addition
            spare = spare - addition
    return np.array([reach] + counts)


def uneven_parts(stream_key, number_of, total, limit, skew):
    if number_of == 2:
        one = jax.random.randint(stream_key, (), max(1, total - limit), min(limit, total - 1) + 1)
        return jnp.stack([one, total - one])
    sizes = jnp.asarray(profile(number_of, total, limit, skew), jnp.int32)
    couples = (number_of - 1) // 2
    donor, taker = sizes[1:1 + 2 * couples:2], sizes[2:2 + 2 * couples:2]
    margin = jnp.minimum(donor - 1, limit - taker)
    moved = jax.random.randint(jax.random.fold_in(stream_key, 1), (couples,), 0, 1 << 20) % (margin + 1)
    sizes = sizes.at[1:1 + 2 * couples:2].set(donor - moved).at[2:2 + 2 * couples:2].set(taker + moved)
    return sizes[jax.random.permutation(jax.random.fold_in(stream_key, 2), number_of)]


def noise(stream_key, dims, scale, most, cuts=(), kind=jnp.bfloat16):
    values = scale * jax.random.normal(stream_key, dims, jnp.float32)
    if cuts:
        values = values * shard_levels(stream_key, dims, cuts, -0.22, 0.18)
    return jnp.clip(values, -most, most).astype(kind)


def setup_inputs(seed: int = 0) -> dict:
    splits = jax.random.split(jax.random.key(seed), 9)
    return {
        "density_factor": noise(splits[0], (NP, RANK), (RANK ** -0.5), 0.25, ((0, 32), (1, 8))),
        "hole_factor": noise(splits[1], (NP, RANK), (RANK ** -0.5), 0.25, ((0, 32), (1, 8))),
        "ph_factor": noise(splits[2], (NP, RANK), (RANK ** -0.5), 0.25, ((0, 32), (1, 8))),
        "hamiltonian": draw_hamiltonian(jax.random.fold_in(splits[8], 71), 0),
        "multiplier_q": draw_multiplier_q(jax.random.fold_in(splits[8], 71), 0),
        "multiplier_g": draw_multiplier_g(jax.random.fold_in(splits[8], 71), 0),
        "ph_perm": draw_ph_perm(jax.random.fold_in(splits[8], 71), 0),
        "block_lengths": uneven_parts(splits[7], SEGS, NP, MOSTLEN, 2).astype(jnp.int32),
    }


shift_value = 2.0
penalty = 2.5


def block_means(values, lengths):
    offsets = jnp.cumsum(lengths).astype(jnp.int32)
    positions = jnp.arange(values.shape[0], dtype=jnp.int32)
    segment = jnp.sum((positions[:, None] >= offsets[None, :]).astype(jnp.int32), axis=1).astype(jnp.int32)
    member = (segment[:, None] == jnp.arange(lengths.shape[0], dtype=jnp.int32)[None, :]).astype(values.dtype)
    means = jnp.sum(member * values[:, None], axis=0) / lengths.astype(values.dtype)
    return jnp.sum(member * means[None, :], axis=1)


def reference(density_factor, hole_factor, ph_factor, hamiltonian, multiplier_q, multiplier_g, ph_perm, block_lengths):
    density_ph = jnp.take(density_factor, ph_perm, axis=0)
    pair_cat = jnp.concatenate([density_factor, hole_factor], axis=1)
    ph_cat = jnp.concatenate([density_ph, ph_factor], axis=1)
    identity = jnp.eye(NP, dtype=jnp.float32)
    diag_density = jnp.sum(jnp.square(density_factor.astype(jnp.float32)), axis=1)
    shifted = 2.0 * block_means(diag_density, block_lengths)
    shifted_ph = jnp.take(shifted, ph_perm)
    resid_q = shift_value * identity - jnp.dot(pair_cat, pair_cat.T, preferred_element_type=jnp.float32)
    resid_g = shifted_ph[:, None] * identity - jnp.dot(ph_cat, ph_cat.T, preferred_element_type=jnp.float32)
    full_q = multiplier_q.astype(jnp.float32) + penalty * resid_q
    full_g = multiplier_g.astype(jnp.float32) + penalty * resid_g
    weight_q = full_q.astype(jnp.bfloat16)
    weight_g = full_g.astype(jnp.bfloat16)
    weight_pair = jnp.zeros((NP,), jnp.float32).at[ph_perm].set(jnp.diagonal(full_g))
    scaling = 2.0 * block_means(weight_pair, block_lengths)
    energy = jnp.dot(hamiltonian, density_factor, preferred_element_type=jnp.float32)
    pair_term = jnp.dot(weight_q, pair_cat, preferred_element_type=jnp.float32)
    ph_term = jnp.dot(weight_g, ph_cat, preferred_element_type=jnp.float32)
    returned = jnp.zeros((NP, RANK), jnp.float32).at[ph_perm].set(ph_term[:, :RANK])
    grad_density = 2.0 * energy - 2.0 * pair_term[:, :RANK] + 2.0 * scaling[:, None] * density_factor.astype(jnp.float32) - 2.0 * returned
    grad_hole = -2.0 * pair_term[:, RANK:]
    grad_ph = -2.0 * ph_term[:, RANK:]
    return (grad_density, grad_hole, grad_ph)
```

```python
import jax
import jax.numpy as jnp
from jax import lax
from jax.sharding import PartitionSpec as P

shift_value = 2.0
penalty = 2.5
both = ("row", "col")
f32 = jnp.float32
bf16 = jnp.bfloat16


def contract_rows(left, right):
    return lax.dot_general(left, right, (((1,), (1,)), ((), ())), preferred_element_type=f32)


def pick(one_hot, values):
    return jnp.dot(
        one_hot.astype(values.dtype),
        values,
        precision=lax.Precision.HIGHEST if values.dtype == f32 else None,
        preferred_element_type=f32,
    ).astype(values.dtype)


def digit(axis):
    name, stride, length = axis
    return lax.axis_index(name) // stride % length


def turn(x, axis, step):
    name, stride, length = axis
    pairs = []
    for i in range(lax.axis_size(name)):
        d = i // stride % length
        pairs.append((i, i + ((d + step) % length - d) * stride))
    return lax.ppermute(x, name, pairs)


def steps_of(axis):
    return {2: (1,), 4: (1, -1, 2)}[axis[2]]


def gather_digit(x, axis):
    here = digit(axis)
    moved = [(0, x)] + [(-s, turn(x, axis, s)) for s in steps_of(axis)]
    out = jnp.zeros((axis[2],) + x.shape, x.dtype)
    for offset, value in moved:
        out = lax.dynamic_update_slice_in_dim(out, value[None], (here + offset) % axis[2], 0)
    return out


def sum_digit(x, axis):
    total = x
    for s in steps_of(axis):
        total = total + turn(x, axis, s)
    return total


z_hi, x_axis, core = ("row", 8, 4), ("row", 2, 4), ("row", 1, 2)
z_lo, y_axis = ("col", 4, 2), ("col", 1, 4)


def gather_rows(x):
    out = gather_digit(x, z_hi)
    out = gather_digit(out, x_axis)
    out = gather_digit(out, core)
    return jnp.transpose(out, (2, 1, 0) + tuple(range(3, out.ndim))).reshape((-1,) + x.shape)


def gather_cols(x):
    out = gather_digit(gather_digit(x, z_lo), y_axis)
    return jnp.swapaxes(out, 0, 1).reshape((-1,) + x.shape)


def sum_all(x):
    for axis in (core, z_lo, x_axis, y_axis, z_hi):
        x = sum_digit(x, axis)
    return x


def local(
    density_factor,
    hole_factor,
    ph_factor,
    hamiltonian,
    multiplier_q,
    multiplier_g,
    ph_perm,
    block_lengths,
):
    rows, cols = lax.axis_size("row"), lax.axis_size("col")
    row_index = lax.axis_index("row")
    col_index = lax.axis_index("col")
    block, part = density_factor.shape
    width = multiplier_q.shape[1]
    per = width // block
    each = width // rows
    row_ids = row_index * block + jnp.arange(block, dtype=jnp.int32)
    col_ids = col_index * width + jnp.arange(width, dtype=jnp.int32)
    on_diag = row_ids[:, None] == col_ids[None, :]
    mine = lax.dynamic_slice_in_dim(ph_perm, row_index * block, block)
    wide = lax.dynamic_slice_in_dim(ph_perm, col_index * width, width)

    ends = jnp.sum(
        jnp.where(
            jnp.arange(block_lengths.shape[0])[:, None] >= jnp.arange(block_lengths.shape[0])[None, :],
            block_lengths[None, :],
            0,
        ),
        axis=1,
    )
    starts = ends - block_lengths
    in_segment = ((row_ids[:, None] >= starts) & (row_ids[:, None] < ends)).astype(f32)
    ph_segment = ((mine[:, None] >= starts) & (mine[:, None] < ends)).astype(f32)
    density_sq = jnp.sum(jnp.square(density_factor.astype(f32)), axis=1)
    ph_sq = jnp.sum(jnp.square(ph_factor.astype(f32)), axis=1)
    mult_diag = jnp.sum(jnp.where(on_diag, multiplier_g.astype(f32), 0.0), axis=1)
    stats = jnp.stack(
        [
            jnp.sum(in_segment * density_sq[:, None], axis=0),
            jnp.sum(ph_segment * (mult_diag - penalty * ph_sq)[:, None], axis=0),
        ]
    )
    stats = sum_all(stats) / block_lengths.astype(f32)
    shift_rows = jnp.sum(ph_segment * (2.0 * stats[0]), axis=1)
    scale_rows = jnp.sum(in_segment * (2.0 * (stats[1] + penalty * stats[0])), axis=1)

    places = jnp.arange(rows * block, dtype=jnp.int32)
    target = jnp.sum(jnp.where(ph_perm[None, :] == row_ids[:, None], places[None, :], 0), axis=1)
    order = jnp.sum((target[None, :] < target[:, None]).astype(jnp.int32), axis=1)
    send = jnp.arange(block, dtype=jnp.int32)[:, None] == order[None, :]

    def arrival(ids, share):
        source = ids // block
        n = ids.shape[0]
        place = jnp.arange(n, dtype=jnp.int32)
        earlier = (source[None, :] == source[:, None]) & (place[None, :] < place[:, None])
        slot = source * share + jnp.sum(earlier.astype(jnp.int32), axis=1)
        return slot[:, None] == place[None, :]

    receive = arrival(mine, block // rows)
    receive_wide = arrival(wide, each)
    leaving = pick(send, density_factor)

    pair_local = jnp.concatenate([density_factor, hole_factor], axis=1)
    moved = lax.ppermute(
        jnp.concatenate([pair_local, ph_factor], axis=1),
        both,
        [
            (r * cols + c, ((r % per) * cols + c) * cols + r // per)
            for r in range(rows)
            for c in range(cols)
        ],
    )
    by_col = lax.all_to_all(leaving.reshape(cols, each, part), "col", 0, 0)
    density_piece = jnp.swapaxes(by_col, 0, 1).reshape(each * cols * part // part, part)
    column = gather_rows(jnp.concatenate([moved, density_piece], axis=1))
    column = column.reshape(per, cols, block, 4 * part)
    pair_col = jnp.swapaxes(column[..., : 2 * part], 1, 2).reshape(width, cols * 2 * part)
    hole_col = jnp.swapaxes(column[..., 2 * part : 3 * part], 1, 2).reshape(width, cols * part)
    density_col = pick(receive_wide, column[..., 3 * part :].reshape(width, cols * part))

    incoming = lax.all_to_all(leaving, "row", 0, 0, tiled=True)
    density_ph = pick(receive, incoming)
    row_whole = gather_cols(jnp.concatenate([pair_local, ph_factor, density_ph], axis=1))
    row_whole = jnp.swapaxes(row_whole, 0, 1)
    pair_row = row_whole[..., : 2 * part].reshape(block, -1)
    hole_row = row_whole[..., 2 * part : 3 * part].reshape(block, -1)
    density_row = row_whole[..., 3 * part :].reshape(block, -1)

    gram_q = contract_rows(pair_row, pair_col)
    gram_g = contract_rows(density_row, density_col) + contract_rows(hole_row, hole_col)
    resid_q = jnp.where(on_diag, shift_value, 0.0) - gram_q
    resid_g = jnp.where(on_diag, shift_rows[:, None], 0.0) - gram_g
    weight_q = (multiplier_q.astype(f32) + penalty * resid_q).astype(bf16)
    weight_g = (multiplier_g.astype(f32) + penalty * resid_g).astype(bf16)

    energy = jnp.dot(hamiltonian, pair_col, preferred_element_type=f32).reshape(block, cols, -1)
    pair_term = jnp.dot(weight_q, pair_col, preferred_element_type=f32).reshape(block, cols, -1)
    first = jnp.arange(2 * part) < part
    pair_part = jnp.where(first, 2.0 * energy, 0.0) - 2.0 * pair_term
    density_term = jnp.dot(weight_g, density_col, preferred_element_type=f32).reshape(block, cols, -1)
    hole_term = jnp.dot(weight_g, hole_col, preferred_element_type=f32).reshape(block, cols, -1)
    parts = jnp.swapaxes(
        jnp.concatenate([pair_part, -2.0 * density_term, -2.0 * hole_term], axis=2), 0, 1
    )
    done = jnp.sum(lax.all_to_all(parts, "col", 0, 0), axis=0)

    back = pick(receive.T, done[:, 2 * part : 3 * part])
    returned = pick(send.T, lax.all_to_all(back, "row", 0, 0, tiled=True))
    grad_density = (
        done[:, :part] + 2.0 * scale_rows[:, None] * density_factor.astype(f32) + returned
    )
    return (grad_density, done[:, part : 2 * part], done[:, 3 * part :])


def solution(mesh):
    return jax.shard_map(
        local,
        mesh=mesh,
        in_specs=(
            P("row", "col"),
            P("row", "col"),
            P("row", "col"),
            P("row", "col"),
            P("row", "col"),
            P("row", "col"),
            P(),
            P(),
        ),
        out_specs=(P("row", "col"), P("row", "col"), P("row", "col")),
        check_vma=False,
    )
```

```python
import functools
import jax
import jax.numpy as jnp
from jax import lax
from jax.experimental import pallas as pl
from jax.experimental.pallas import tpu as pltpu
from jax.sharding import PartitionSpec as P

shift_value = 2.0
penalty = 2.5
both = ("row", "col")
f32 = jnp.float32
bf16 = jnp.bfloat16
lanes = 128
extra = 16


def pick(one_hot, values):
    return jnp.dot(
        one_hot.astype(values.dtype),
        values,
        precision=lax.Precision.HIGHEST if values.dtype == f32 else None,
        preferred_element_type=f32,
    ).astype(values.dtype)


z_hi, x_axis, core = ("row", 8, 4), ("row", 2, 4), ("row", 1, 2)
z_lo, y_axis = ("col", 4, 2), ("col", 1, 4)
offsets = {2: (0, 1), 4: (0, -1, 1, 2)}


def digit(axis):
    name, stride, length = axis
    return lax.axis_index(name) // stride % length


def turn(x, axis, step):
    name, stride, length = axis
    pairs = []
    for i in range(lax.axis_size(name)):
        d = i // stride % length
        pairs.append((i, i + ((d + step) % length - d) * stride))
    return lax.ppermute(x, name, pairs)


def gather_digit(x, axis):
    moved = [turn(x, axis, -offset) for offset in offsets[axis[2]][1:]]
    return jnp.stack([x] + moved)


def gather_rows(x):
    out = gather_digit(gather_digit(x, z_hi), x_axis)
    out = out.reshape((-1,) + x.shape)
    return out, turn(out, core, 1)


def gather_cols(x):
    out = gather_digit(gather_digit(x, z_lo), y_axis)
    return out.reshape((-1,) + x.shape)


def to_column(x, rows, cols, per):
    return lax.ppermute(
        x,
        both,
        [
            (r * cols + c, ((r % per) * cols + c) * cols + r // per)
            for r in range(rows)
            for c in range(cols)
        ],
    )


def three_parts(x):
    high = lax.reduce_precision(x, 8, 7)
    middle = lax.reduce_precision(x - high, 8, 7)
    low = x - high - middle
    return jnp.stack([high, middle, low]).astype(bf16)


def three_sum(parts):
    return parts[0] + parts[1] + parts[2]


def weights_kernel(block, width, is_q, *refs):
    if is_q:
        place, own, other, around, multiplier, hamiltonian, out, right, left = refs
    else:
        (place, own, other, around, multiplier, segments, ph_segments, lengths, out, scale, right, left) = refs
    zh, xx, cc, zl, yy = (place[i] for i in range(5))
    ids = []
    for xr, xo in enumerate(offsets[4]):
        for cr in range(2):
            k = xr * 2 + cr
            source = own if cr == 0 else other
            c = lax.rem(xx + xo + 4, 4) * 2 + (cc if cr == 0 else 1 - cc)
            ids.append(c)
            for zr, zo in enumerate(offsets[4]):
                j = lax.rem(zh + zo + 4, 4)
                right[pl.ds(pl.multiple_of(j * block, block), block), k * lanes : (k + 1) * lanes] = source[
                    xr * 4 + zr, :block, :
                ]
            dz = jnp.where(c // 4 == zl, 0, 1)
            dy = lax.rem(lax.rem(c, 4) - yy + 4, 4)
            dy = jnp.where(dy == 0, 0, jnp.where(dy == 3, 1, dy + 1))
            left[:, k * lanes : (k + 1) * lanes] = around[dy * 2 + dz, :block, :]
    gram = lax.dot_general(
        left[...], right[...], (((1,), (1,)), ((), ())), preferred_element_type=f32
    )
    row = lax.broadcasted_iota(jnp.int32, (block, width), 0)
    col = lax.broadcasted_iota(jnp.int32, (block, width), 1)
    on_diag = row + ((zh * 8 + xx * 2 + cc) * block - (zl * 4 + yy) * width) == col
    if is_q:
        diagonal = shift_value
    else:
        total = jnp.zeros((extra, lanes), f32)
        for source in (own, other):
            for b in range(16):
                total = total + source[b, block:, :].astype(f32)
        mean_d = (total[0:1] + total[1:2] + total[2:3]) / lengths[...]
        mean_u = (total[3:4] + total[4:5] + total[5:6]) / lengths[...]
        diagonal = jnp.sum(ph_segments[...] * (2.0 * mean_d), axis=1, keepdims=True)
        scale[...] = jnp.sum(
            segments[...] * (2.0 * (mean_u + penalty * mean_d)), axis=1, keepdims=True
        )
    resid = jnp.where(on_diag, diagonal, 0.0) - gram
    weight = (multiplier[...].astype(f32) + penalty * resid).astype(bf16)
    term = -2.0 * jnp.dot(weight, right[...], preferred_element_type=f32)
    if is_q:
        energy = 2.0 * jnp.dot(hamiltonian[...], right[...], preferred_element_type=f32)
        lane = lax.broadcasted_iota(jnp.int32, energy.shape, 1)
        term = term + jnp.where(lax.rem(lane, lanes) < lanes // 2, energy, 0.0)
    for k, c in enumerate(ids):
        out[c] = term[:, k * lanes : (k + 1) * lanes]


def apply_weights(is_q, *args):
    block, width = args[4].shape
    cols = 8
    shapes = [jax.ShapeDtypeStruct((cols, block, lanes), f32)]
    if not is_q:
        shapes.append(jax.ShapeDtypeStruct((block, 1), f32))
    vmem = pl.BlockSpec(memory_space=pltpu.VMEM)
    return pl.pallas_call(
        functools.partial(weights_kernel, block, width, is_q),
        out_shape=shapes,
        in_specs=[pl.BlockSpec(memory_space=pltpu.SMEM)] + [vmem] * (len(args) - 1),
        out_specs=[vmem] * len(shapes),
        scratch_shapes=[
            pltpu.VMEM((width, cols * lanes), bf16),
            pltpu.VMEM((block, cols * lanes), bf16),
        ],
        compiler_params=pltpu.CompilerParams(vmem_limit_bytes=40 * 1024 * 1024),
        name="weights_q" if is_q else "weights_g",
    )(*args)


def local(
    density_factor,
    hole_factor,
    ph_factor,
    hamiltonian,
    multiplier_q,
    multiplier_g,
    ph_perm,
    block_lengths,
):
    rows, cols = lax.axis_size("row"), lax.axis_size("col")
    row_index = lax.axis_index("row")
    col_index = lax.axis_index("col")
    block, part = density_factor.shape
    width = multiplier_q.shape[1]
    per = width // block
    place = jnp.stack([digit(axis) for axis in (z_hi, x_axis, core, z_lo, y_axis)]).astype(jnp.int32)
    row_ids = row_index * block + jnp.arange(block, dtype=jnp.int32)
    col_ids = col_index * width + jnp.arange(width, dtype=jnp.int32)
    on_diag = row_ids[:, None] == col_ids[None, :]
    mine = lax.dynamic_slice_in_dim(ph_perm, row_index * block, block)

    places = jnp.arange(rows * block, dtype=jnp.int32)
    target = jnp.sum(jnp.where(ph_perm[None, :] == row_ids[:, None], places[None, :], 0), axis=1)
    order = jnp.sum((target[None, :] < target[:, None]).astype(jnp.int32), axis=1)
    spot = jnp.arange(block, dtype=jnp.int32)
    send = spot[:, None] == order[None, :]
    source = mine // block
    earlier = (source[None, :] == source[:, None]) & (spot[None, :] < spot[:, None])
    slot = source * (block // rows) + jnp.sum(earlier.astype(jnp.int32), axis=1)
    receive = slot[:, None] == spot[None, :]

    lengths = jnp.concatenate(
        [block_lengths, jnp.zeros((lanes - block_lengths.shape[0],), jnp.int32)]
    )
    lane = jnp.arange(lanes, dtype=jnp.int32)
    ends = jnp.sum(jnp.where(lane[:, None] >= lane[None, :], lengths[None, :], 0), axis=1)
    starts = ends - lengths
    segments = ((row_ids[:, None] >= starts) & (row_ids[:, None] < ends)).astype(f32)
    ph_segments = ((mine[:, None] >= starts) & (mine[:, None] < ends)).astype(f32)
    density_sq = jnp.sum(jnp.square(density_factor.astype(f32)), axis=1)
    ph_sq = jnp.sum(jnp.square(ph_factor.astype(f32)), axis=1)
    mult_diag = jnp.sum(jnp.where(on_diag, multiplier_g.astype(f32), 0.0), axis=1)
    stat_d = jnp.sum(segments * density_sq[:, None], axis=0)
    stat_u = jnp.sum(ph_segments * (mult_diag - penalty * ph_sq)[:, None], axis=0)

    def stat_rows(d, u):
        rest = jnp.zeros((extra - 6, lanes), bf16)
        return jnp.concatenate([three_parts(d), three_parts(u), rest])

    pair_local = jnp.concatenate([density_factor, hole_factor], axis=1)
    own_q, other_q = gather_rows(to_column(pair_local, rows, cols, per))
    around_q = gather_cols(jnp.concatenate([pair_local, stat_rows(stat_d, stat_u)]))
    stats = jnp.sum(around_q[:, block:].astype(f32), axis=0)
    stats = stat_rows(three_sum(stats[0:3]), three_sum(stats[3:6]))

    leaving = pick(send, density_factor)
    density_ph = pick(receive, lax.all_to_all(leaving, "row", 0, 0, tiled=True))
    ph_local = jnp.concatenate([density_ph, ph_factor], axis=1)
    own_g, other_g = gather_rows(jnp.concatenate([to_column(ph_local, rows, cols, per), stats]))
    around_g = gather_cols(ph_local)

    (parts_q,) = apply_weights(True, place, own_q, other_q, around_q, multiplier_q, hamiltonian)
    parts_g, scale_rows = apply_weights(
        False,
        place,
        own_g,
        other_g,
        around_g,
        multiplier_g,
        segments,
        ph_segments,
        jnp.maximum(lengths, 1).astype(f32)[None, :],
    )
    done_g = jnp.sum(lax.all_to_all(parts_g, "col", 0, 0), axis=0)
    done_q = jnp.sum(lax.all_to_all(parts_q, "col", 0, 0), axis=0)

    back = pick(receive.T, done_g[:, :part])
    returned = pick(send.T, lax.all_to_all(back, "row", 0, 0, tiled=True))
    grad_density = done_q[:, :part] + 2.0 * scale_rows * density_factor.astype(f32) + returned
    return (grad_density, done_q[:, part:], done_g[:, part:])


def solution(mesh):
    return jax.shard_map(
        local,
        mesh=mesh,
        in_specs=(
            P("row", "col"),
            P("row", "col"),
            P("row", "col"),
            P("row", "col"),
            P("row", "col"),
            P("row", "col"),
            P(),
            P(),
        ),
        out_specs=(P("row", "col"), P("row", "col"), P("row", "col")),
        check_vma=False,
    )
```

```python
import jax
import jax.numpy as jnp
from jax import lax
from jax.experimental import pallas as pl
from jax.experimental.pallas import tpu as pltpu
from jax.sharding import PartitionSpec as P

shift_value = 2.0
penalty = 2.5
both = ("row", "col")
f32 = jnp.float32
bf16 = jnp.bfloat16
i32 = jnp.int32
lanes = 128
half = 64
group = 8
extra = 16
vmem = pl.BlockSpec(memory_space=pltpu.VMEM)
hbm = pl.BlockSpec(memory_space=pltpu.MemorySpace.HBM)
smem = pl.BlockSpec(memory_space=pltpu.SMEM)


z_hi, x_axis, core = ("row", 8, 4), ("row", 2, 4), ("row", 1, 2)
z_lo, y_axis = ("col", 4, 2), ("col", 1, 4)
offsets = (0, -1, 1, 2)


def digit(axis):
    name, stride, length = axis
    return lax.axis_index(name) // stride % length


def turn(x, axis, step):
    name, stride, length = axis
    pairs = []
    for i in range(lax.axis_size(name)):
        d = i // stride % length
        pairs.append((i, i + ((d + step) % length - d) * stride))
    return lax.ppermute(x, name, pairs)


def gather_digit(x, axis):
    return jnp.stack([x] + [turn(x, axis, -offset) for offset in offsets[1:]])


def gather_cols(x):
    two = jnp.stack([x, turn(x, z_lo, 1)])
    return [two] + [turn(two, y_axis, -offset) for offset in offsets[1:]]


def to_column(x, rows, cols, per):
    pairs = []
    for r in range(rows):
        for c in range(cols):
            pairs.append((r * cols + c, ((r % per) * cols + c) * cols + r // per))
    return lax.ppermute(x, both, pairs)


def iota(shape, axis):
    return lax.broadcasted_iota(i32, shape, axis)


def column_of(row, n):
    return jnp.sum(jnp.where(iota((n, n), 0) == iota((n, n), 1), row, 0), axis=1, keepdims=True)


def row_of(column, n):
    return jnp.sum(jnp.where(iota((n, n), 0) == iota((n, n), 1), column, 0), axis=0, keepdims=True)


def over_block(x):
    return ((x >> 6) * 21846) >> 16


def one_hot(condition, dtype=bf16):
    return jnp.where(condition, 1.0, 0.0).astype(dtype)


def transposed_dot(left, right):
    return lax.dot_general(left, right, (((1,), (1,)), ((), ())), preferred_element_type=f32)


def exact_dot(left, right):
    return jnp.dot(left, right, precision=lax.Precision.HIGHEST, preferred_element_type=f32)


def three_parts(value):
    pieces = []
    for _ in range(3):
        piece = value.astype(bf16).astype(f32)
        pieces.append(piece)
        value = value - piece
    return pieces


def block_of(perm, b, n):
    at = lax.div(b * n, lanes)
    two = jnp.concatenate([perm[pl.ds(at, 1), :], perm[pl.ds(at + 1, 1), :]], axis=1)
    return jnp.where(b * n == at * lanes, two[:, :n], two[:, lanes // 2 : lanes // 2 + n])


def rank_in_block(mine, n):
    column = column_of(mine, n)
    source = over_block(column)
    earlier = (over_block(mine) == source) & (iota((n, n), 1) < iota((n, n), 0))
    return column, source, jnp.sum(jnp.where(earlier, 1, 0), axis=1, keepdims=True)


def routes_kernel(
    place,
    perm,
    lengths,
    density_far,
    hole_far,
    ph_far,
    multiplier_far,
    leaving,
    local,
    send,
    receive,
    receive_across,
    segments,
    ph_segments,
    density,
    hole,
    ph,
    multiplier,
    sems,
):
    fars = (density_far, hole_far, ph_far, multiplier_far)
    copies = [
        pltpu.make_async_copy(far, here, sems.at[i])
        for i, (far, here) in enumerate(zip(fars, (density, hole, ph, multiplier)))
    ]
    for copy in copies:
        copy.start()
    part, block = density.shape
    width = multiplier.shape[1]
    padded = receive_across.shape[0]
    rows = padded // group
    r, c = place[3], place[4]
    square = (block, block)
    ids = r * block + iota((block, 1), 0)
    target = jnp.zeros((block, lanes), i32)
    for g in range(perm.shape[0]):
        target = target + jnp.where(
            perm[g : g + 1, :] == ids, iota((block, lanes), 1) + g * lanes, 0
        )
    target = jnp.sum(target, axis=1, keepdims=True)
    target_row = row_of(target, block)
    spot = jnp.sum(jnp.where(target < target_row, 1, 0), axis=0, keepdims=True)
    spot = spot + (group - block // rows) * over_block(target_row)
    send[...] = one_hot(iota((block, padded), 1) == column_of(spot, block))

    mine_column, source, rank = rank_in_block(block_of(perm, r, block), block)
    slot = source * group + rank
    receive[...] = one_hot(iota((block, padded), 1) == slot)
    receive_across[...] = one_hot(iota((padded, block), 0) == row_of(slot, block))

    for copy in copies:
        copy.wait()
    eye = one_hot(iota(square, 0) == iota(square, 1))
    blank = jnp.zeros((lanes - part, block), bf16)
    pair = transposed_dot(eye, jnp.concatenate([density[...], hole[...]], axis=0))
    tail = transposed_dot(eye, jnp.concatenate([blank, ph[...]], axis=0))
    local[0] = pair.astype(bf16)
    local[1] = tail.astype(bf16)
    gone = transposed_dot(
        one_hot(iota((padded, block), 0) == spot), jnp.concatenate([density[...], blank], axis=0)
    )

    sizes = jnp.concatenate(
        [lengths[...].astype(f32), jnp.zeros((1, lanes - lengths.shape[1]), f32)], axis=1
    )
    upper = one_hot(iota((lanes, lanes), 0) <= iota((lanes, lanes), 1))
    ends = jnp.dot(
        jnp.broadcast_to(sizes, (8, lanes)).astype(bf16), upper, preferred_element_type=f32
    )[0:1]
    starts = ends - sizes
    positions = ids.astype(f32)
    ph_positions = mine_column.astype(f32)
    inside = one_hot((positions >= starts) & (positions < ends), f32)
    ph_inside = one_hot((ph_positions >= starts) & (ph_positions < ends), f32)
    segments[...] = inside
    ph_segments[...] = ph_inside
    first = iota((block, lanes), 1) < half
    density_sq = jnp.sum(jnp.where(first, pair * pair, 0.0), axis=1, keepdims=True)
    on_diag = iota((block, width), 0) + (r * block - c * width) == iota((block, width), 1)
    share = jnp.sum(jnp.where(on_diag, multiplier[...].astype(f32), 0.0), axis=1, keepdims=True)
    share = share - penalty * jnp.sum(tail * tail, axis=1, keepdims=True)
    pieces = three_parts(jnp.sum(inside * density_sq, axis=0, keepdims=True)) + three_parts(
        jnp.sum(ph_inside * share, axis=0, keepdims=True)
    )
    at = iota((padded, lanes), 0) & (group - 1)
    late = iota((padded, lanes), 1) >= half
    for row, piece in enumerate(pieces):
        gone = jnp.where((at == row) & late, pltpu.roll(piece, half, 1), gone)
    leaving[...] = gone.astype(bf16)


def rows_kernel(incoming, receive, local, body, longer):
    block = local.shape[1]
    values = jnp.dot(receive[...], incoming[...], preferred_element_type=f32)
    values = jnp.where(iota(values.shape, 1) < half, values, local[1].astype(f32)).astype(bf16)
    sums = jnp.zeros((group, lanes), f32)
    arrived = incoming[...].astype(f32)
    for g in range(arrived.shape[0] // group):
        sums = sums + arrived[g * group : (g + 1) * group]
    sums = pltpu.roll(sums, half, 1)
    at = iota((extra, lanes), 0)
    tile = jnp.zeros((extra, lanes), f32)
    for k in range(2):
        value = sums[3 * k : 3 * k + 1] + sums[3 * k + 1 : 3 * k + 2] + sums[3 * k + 2 : 3 * k + 3]
        for i, piece in enumerate(three_parts(value)):
            tile = jnp.where(at == 3 * k + i, piece, tile)
    for out in (body, longer):
        out[:block] = local[0]
        out[block : 2 * block] = values
    longer[2 * block :] = tile.astype(bf16)


def halves_side_by_side(top, bottom, first):
    low = iota(top.shape, 1) < half
    if first:
        return jnp.where(low, top, pltpu.roll(bottom, half, 1))
    return jnp.where(low, pltpu.roll(top, half, 1), bottom)


def rows_again(packed, first):
    turned = pltpu.roll(packed, half, 1)
    return jnp.concatenate([packed, turned] if first else [turned, packed], axis=0)


def sum_parts(parts):
    total = parts[0]
    for k in range(1, parts.shape[0]):
        total = total + parts[k]
    return total


def diagonal_of(place, shape):
    block, width = shape
    return iota(shape, 0) + (place[3] * block - place[4] * width) == iota(shape, 1)


def places_of(place, own, other):
    zh, xx, cc = place[0], place[1], place[2]
    for cr, source in enumerate((own, other)):
        for xr, xo in enumerate(offsets):
            from_col = ((xx + xo) & 3) * 2 + (cc if cr == 0 else 1 - cc)
            for zr, zo in enumerate(offsets):
                yield cr, xr * 4 + zr, source, from_col, (zh + zo) & 3


def column_at(place, y_place, z_place):
    return ((place[4] + offsets[y_place]) & 3) + (((place[4] >> 2) + z_place) & 1) * 4


def fill(place, own, other, around, base, right, left, by_col):
    block = left.shape[0]
    ids = []
    for cr, b, source, from_col, j in places_of(place, own, other):
        k = cr * 4 + b // 4
        right[pl.ds(pl.multiple_of(j * block, block), block), k * lanes : (k + 1) * lanes] = source[
            b, base : base + block, :
        ]
        if b % 4 == 0:
            ids.append(from_col)
    for y_place, source in enumerate(around):
        for z_place in range(2):
            by_col[column_at(place, y_place, z_place)] = source[z_place, base : base + block]
    for k, from_col in enumerate(ids):
        left[:, k * lanes : (k + 1) * lanes] = by_col[from_col]
    return ids


def g_kernel(
    place, own, other, a0, a1, a2, a3, multiplier, segments, ph_segments, lengths,
    out, more, scale, right, left, by_col,
):
    block, width = multiplier.shape
    around = (a0, a1, a2, a3)
    ids = fill(place, own, other, around, block, right, left, by_col)
    sums = jnp.zeros((extra, lanes), f32)
    for source in around:
        for z_place in range(2):
            sums = sums + source[z_place, 2 * block :].astype(f32)
    blank = jnp.ones((1, lanes - lengths.shape[1]), f32)
    sizes = jnp.concatenate([lengths[...].astype(f32), blank], axis=1)
    mean_d = (sums[0:1] + sums[1:2] + sums[2:3]) / sizes
    mean_u = (sums[3:4] + sums[4:5] + sums[5:6]) / sizes
    shifts = jnp.sum(ph_segments[...] * (2.0 * mean_d), axis=1, keepdims=True)
    scale[...] = jnp.sum(
        segments[...] * (2.0 * (mean_u + penalty * mean_d)), axis=1, keepdims=True
    )
    gram = transposed_dot(left[...], right[...])
    resid = jnp.where(diagonal_of(place, multiplier.shape), shifts, 0.0) - gram
    weight = (multiplier[...].astype(f32) + penalty * resid).astype(bf16)
    term = -2.0 * jnp.dot(weight, right[...], preferred_element_type=f32)
    for k, from_col in enumerate(ids):
        top = term[: block // 2, k * lanes : (k + 1) * lanes]
        bottom = term[block // 2 :, k * lanes : (k + 1) * lanes]
        out[from_col] = halves_side_by_side(top, bottom, True)
        more[from_col] = halves_side_by_side(top, bottom, False)


def q_kernel(
    place, own, other, a0, a1, a2, a3, multiplier, hamiltonian, more,
    keep, away, right, left, by_col, by_col_out,
):
    block, width = multiplier.shape
    ids = fill(place, own, other, (a0, a1, a2, a3), 0, right, left, by_col)
    gram = transposed_dot(left[...], right[...])
    resid = jnp.where(diagonal_of(place, multiplier.shape), shift_value, 0.0) - gram
    weight = (multiplier[...].astype(f32) + penalty * resid).astype(bf16)
    term = -2.0 * jnp.dot(weight, right[...], preferred_element_type=f32)
    energy = 2.0 * jnp.dot(hamiltonian[...], right[...], preferred_element_type=f32)
    term = term + jnp.where((iota(energy.shape, 1) & (lanes - 1)) < half, energy, 0.0)
    for k, from_col in enumerate(ids):
        by_col_out[from_col] = term[:, k * lanes : (k + 1) * lanes]
    for z_place, out in enumerate((keep, away)):
        for y_place in range(4):
            from_col = column_at(place, y_place, z_place)
            out[y_place, :block, :] = by_col_out[from_col]
            out[y_place, block:, :] = more[from_col]


def back_kernel(parts, receive_across, back):
    total = rows_again(sum_parts(parts), True)
    back[...] = exact_dot(receive_across[...].astype(f32), total)


def add_kernel(keep, came, *outs):
    for k, out in enumerate(outs):
        out[...] = keep[k] + came[k]


def last_kernel(p0, p1, p2, p3, returned, send, local, scale, density, hole, ph):
    block = local.shape[1]
    total = p0[...] + p1[...] + p2[...] + p3[...]
    ph[...] = rows_again(total[block:], False).T[half:]
    total = total[:block]
    more = exact_dot(send[...].astype(f32), returned[...])
    more = more + 2.0 * scale[...] * local[0].astype(f32)
    total = jnp.where(iota(total.shape, 1) < half, total + more, total).T
    density[...] = total[:half]
    hole[...] = total[half:]


def call(kernel, name, shapes, args, scratch=(), scalars=True, far=(), copies=0, room=8):
    return pl.pallas_call(
        kernel,
        out_shape=[jax.ShapeDtypeStruct(s, d) for s, d in shapes],
        in_specs=[smem] * scalars
        + [hbm if i in far else vmem for i in range(scalars, len(args))],
        out_specs=[vmem] * len(shapes),
        scratch_shapes=[pltpu.VMEM(s, d) for s, d in scratch]
        + [pltpu.SemaphoreType.DMA((copies,))] * (copies > 0),
        compiler_params=pltpu.CompilerParams(vmem_limit_bytes=room * 1024 * 1024),
        name=name,
    )(*args)


def local(
    density_factor,
    hole_factor,
    ph_factor,
    hamiltonian,
    multiplier_q,
    multiplier_g,
    ph_perm,
    block_lengths,
):
    rows, cols = lax.axis_size("row"), lax.axis_size("col")
    block, part = density_factor.shape
    width = multiplier_q.shape[1]
    per = width // block
    padded = rows * group
    place = jnp.stack(
        [digit(axis) for axis in (z_hi, x_axis, core)]
        + [lax.axis_index("row"), lax.axis_index("col")]
    ).astype(i32)
    lengths = block_lengths[None, :]
    perm = ph_perm.reshape(-1, lanes)
    leaving, mine, send, receive, receive_across, segments, ph_segments = call(
        routes_kernel,
        "routes",
        [
            ((padded, lanes), bf16),
            ((2, block, lanes), bf16),
            ((block, padded), bf16),
            ((block, padded), bf16),
            ((padded, block), bf16),
            ((block, lanes), f32),
            ((block, lanes), f32),
        ],
        (place, perm, lengths, density_factor.T, hole_factor.T, ph_factor.T, multiplier_g),
        [((part, block), bf16)] * 3 + [((block, width), bf16)],
        far=(3, 4, 5, 6),
        copies=4,
        room=60,
    )
    incoming = lax.all_to_all(leaving.reshape(rows, group, lanes), "row", 0, 0)
    tall = 2 * block
    body, longer = call(
        rows_kernel,
        "rows",
        [((tall, lanes), bf16), ((tall + extra, lanes), bf16)],
        (incoming.reshape(padded, lanes), receive, mine),
        scalars=False,
    )
    piece = to_column(body, rows, cols, per)
    near = gather_digit(piece, z_hi)
    own = gather_digit(near, x_axis).reshape(16, tall, lanes)
    around = gather_cols(longer)
    own, around = lax.optimization_barrier((own, around))
    other = turn(own, core, 1)
    gathered = (place, own, other, *around)
    shared = [
        ((width, cols * lanes), bf16),
        ((block, cols * lanes), bf16),
        ((cols, block, lanes), bf16),
    ]
    parts_e, parts_f, scale = call(
        g_kernel,
        "weights_g",
        [((cols, block // 2, lanes), f32), ((cols, block // 2, lanes), f32), ((block, 1), f32)],
        (*gathered, multiplier_g, segments, ph_segments, lengths),
        shared,
        room=16,
    )
    long = block + block // 2
    keep, away = call(
        q_kernel,
        "weights_q",
        [((4, long, lanes), f32)] * 2,
        (*gathered, multiplier_q, hamiltonian, parts_f),
        shared + [((cols, block, lanes), f32)],
        room=16,
    )
    parts_e, keep, away = lax.optimization_barrier((parts_e, keep, away))
    sums_e = lax.all_to_all(parts_e, "col", 0, 0)
    came = turn(away, z_lo, 1)
    (back,) = call(
        back_kernel, "back", [((padded, lanes), f32)], (sums_e, receive_across), scalars=False
    )
    returned = lax.all_to_all(back.reshape(rows, group, lanes), "row", 0, 0)
    parts = call(add_kernel, "add", [((long, lanes), f32)] * 4, (keep, came), scalars=False)
    parts = [parts[0]] + [turn(p, y_axis, o) for p, o in zip(parts[1:], offsets[1:])]
    grads = call(
        last_kernel,
        "gradients",
        [((part, block), f32)] * 3,
        (*parts, returned.reshape(padded, lanes), send, mine, scale),
        scalars=False,
    )
    return tuple(g.T for g in grads)


def solution(mesh):
    return jax.shard_map(
        local,
        mesh=mesh,
        in_specs=(
            P("row", "col"),
            P("row", "col"),
            P("row", "col"),
            P("row", "col"),
            P("row", "col"),
            P("row", "col"),
            P(),
            P(),
        ),
        out_specs=(P("row", "col"), P("row", "col"), P("row", "col")),
        check_vma=False,
    )
```

```python
import jax
import jax.numpy as jnp
from jax import lax
from jax.experimental import pallas as pl
from jax.experimental.pallas import tpu as pltpu
from jax.sharding import PartitionSpec as P

shift_value = 2.0
penalty = 2.5
both = ("row", "col")
f32 = jnp.float32
bf16 = jnp.bfloat16
i32 = jnp.int32
lanes = 128
half = 64
group = 8
extra = 16
vmem = pl.BlockSpec(memory_space=pltpu.VMEM)
hbm = pl.BlockSpec(memory_space=pltpu.MemorySpace.HBM)
smem = pl.BlockSpec(memory_space=pltpu.SMEM)


z_hi, x_axis, core = ("row", 8, 4), ("row", 2, 4), ("row", 1, 2)
z_lo, y_axis = ("col", 4, 2), ("col", 1, 4)
offsets = (0, -1, 1, 2)


def digit(axis):
    name, stride, length = axis
    return lax.axis_index(name) // stride % length


def turn(x, axis, step):
    name, stride, length = axis
    pairs = []
    for i in range(lax.axis_size(name)):
        d = i // stride % length
        pairs.append((i, i + ((d + step) % length - d) * stride))
    return lax.ppermute(x, name, pairs)


def around_digit(x, axis):
    return [x] + [turn(x, axis, -offset) for offset in offsets[1:]]


def around_ring(x, axis, way):
    near = turn(x, axis, way)
    other = turn(x, axis, -way)
    far = turn(near, axis, way)
    return [x, near, other, far] if way == 1 else [x, other, near, far]


def gather_cols(x):
    two = jnp.stack([x, turn(x, z_lo, 1)])
    return [two] + [turn(two, y_axis, -offset) for offset in offsets[1:]]


def to_column(x, rows, cols, per):
    pairs = []
    for r in range(rows):
        for c in range(cols):
            pairs.append((r * cols + c, ((r % per) * cols + c) * cols + r // per))
    return lax.ppermute(x, both, pairs)


def iota(shape, axis):
    return lax.broadcasted_iota(i32, shape, axis)


def column_of(row, n):
    return jnp.sum(jnp.where(iota((n, n), 0) == iota((n, n), 1), row, 0), axis=1, keepdims=True)


def row_of(column, n):
    return jnp.sum(jnp.where(iota((n, n), 0) == iota((n, n), 1), column, 0), axis=0, keepdims=True)


def over_block(x):
    return ((x >> 6) * 21846) >> 16


def one_hot(condition, dtype=bf16):
    return jnp.where(condition, 1.0, 0.0).astype(dtype)


def transposed_dot(left, right):
    return lax.dot_general(left, right, (((1,), (1,)), ((), ())), preferred_element_type=f32)


def exact_dot(left, right):
    return jnp.dot(left, right, precision=lax.Precision.HIGHEST, preferred_element_type=f32)


def three_parts(value):
    pieces = []
    for _ in range(3):
        piece = value.astype(bf16).astype(f32)
        pieces.append(piece)
        value = value - piece
    return pieces


def block_of(perm, b, n):
    at = lax.div(b * n, lanes)
    two = jnp.concatenate([perm[pl.ds(at, 1), :], perm[pl.ds(at + 1, 1), :]], axis=1)
    return jnp.where(b * n == at * lanes, two[:, :n], two[:, lanes // 2 : lanes // 2 + n])


def rank_in_block(mine, n):
    column = column_of(mine, n)
    source = over_block(column)
    earlier = (over_block(mine) == source) & (iota((n, n), 1) < iota((n, n), 0))
    return column, source, jnp.sum(jnp.where(earlier, 1, 0), axis=1, keepdims=True)


def routes_kernel(
    place,
    perm,
    lengths,
    density_far,
    hole_far,
    ph_far,
    multiplier_far,
    leaving,
    local,
    send,
    receive,
    receive_across,
    segments,
    ph_segments,
    density,
    hole,
    ph,
    multiplier,
    sems,
):
    fars = (density_far, hole_far, ph_far, multiplier_far)
    copies = [
        pltpu.make_async_copy(far, here, sems.at[i])
        for i, (far, here) in enumerate(zip(fars, (density, hole, ph, multiplier)))
    ]
    for copy in copies:
        copy.start()
    part, block = density.shape
    width = multiplier.shape[1]
    padded = receive_across.shape[0]
    rows = padded // group
    r, c = place[3], place[4]
    square = (block, block)
    ids = r * block + iota((block, 1), 0)
    target = jnp.zeros((block, lanes), i32)
    for g in range(perm.shape[0]):
        target = target + jnp.where(
            perm[g : g + 1, :] == ids, iota((block, lanes), 1) + g * lanes, 0
        )
    target = jnp.sum(target, axis=1, keepdims=True)
    target_row = row_of(target, block)
    spot = jnp.sum(jnp.where(target < target_row, 1, 0), axis=0, keepdims=True)
    spot = spot + (group - block // rows) * over_block(target_row)
    send[...] = one_hot(iota((block, padded), 1) == column_of(spot, block))

    mine_column, source, rank = rank_in_block(block_of(perm, r, block), block)
    slot = source * group + rank
    receive[...] = one_hot(iota((block, padded), 1) == slot)
    receive_across[...] = one_hot(iota((padded, block), 0) == row_of(slot, block))

    for copy in copies:
        copy.wait()
    eye = one_hot(iota(square, 0) == iota(square, 1))
    blank = jnp.zeros((lanes - part, block), bf16)
    pair = transposed_dot(eye, jnp.concatenate([density[...], hole[...]], axis=0))
    tail = transposed_dot(eye, jnp.concatenate([blank, ph[...]], axis=0))
    local[0] = pair.astype(bf16)
    local[1] = tail.astype(bf16)
    gone = transposed_dot(
        one_hot(iota((padded, block), 0) == spot), jnp.concatenate([density[...], blank], axis=0)
    )

    sizes = jnp.concatenate(
        [lengths[...].astype(f32), jnp.zeros((1, lanes - lengths.shape[1]), f32)], axis=1
    )
    upper = one_hot(iota((lanes, lanes), 0) <= iota((lanes, lanes), 1))
    ends = jnp.dot(
        jnp.broadcast_to(sizes, (8, lanes)).astype(bf16), upper, preferred_element_type=f32
    )[0:1]
    starts = ends - sizes
    positions = ids.astype(f32)
    ph_positions = mine_column.astype(f32)
    inside = one_hot((positions >= starts) & (positions < ends), f32)
    ph_inside = one_hot((ph_positions >= starts) & (ph_positions < ends), f32)
    segments[...] = inside
    ph_segments[...] = ph_inside
    first = iota((block, lanes), 1) < half
    density_sq = jnp.sum(jnp.where(first, pair * pair, 0.0), axis=1, keepdims=True)
    on_diag = iota((block, width), 0) + (r * block - c * width) == iota((block, width), 1)
    share = jnp.sum(jnp.where(on_diag, multiplier[...].astype(f32), 0.0), axis=1, keepdims=True)
    share = share - penalty * jnp.sum(tail * tail, axis=1, keepdims=True)
    pieces = three_parts(jnp.sum(inside * density_sq, axis=0, keepdims=True)) + three_parts(
        jnp.sum(ph_inside * share, axis=0, keepdims=True)
    )
    at = iota((padded, lanes), 0) & (group - 1)
    late = iota((padded, lanes), 1) >= half
    for row, piece in enumerate(pieces):
        gone = jnp.where((at == row) & late, pltpu.roll(piece, half, 1), gone)
    leaving[...] = gone.astype(bf16)


def rows_kernel(incoming, receive, local, body, longer):
    block = local.shape[1]
    values = jnp.dot(receive[...], incoming[...], preferred_element_type=f32)
    values = jnp.where(iota(values.shape, 1) < half, values, local[1].astype(f32)).astype(bf16)
    sums = jnp.zeros((group, lanes), f32)
    arrived = incoming[...].astype(f32)
    for g in range(arrived.shape[0] // group):
        sums = sums + arrived[g * group : (g + 1) * group]
    sums = pltpu.roll(sums, half, 1)
    at = iota((extra, lanes), 0)
    tile = jnp.zeros((extra, lanes), f32)
    for k in range(2):
        value = sums[3 * k : 3 * k + 1] + sums[3 * k + 1 : 3 * k + 2] + sums[3 * k + 2 : 3 * k + 3]
        for i, piece in enumerate(three_parts(value)):
            tile = jnp.where(at == 3 * k + i, piece, tile)
    for out in (body, longer):
        out[:block] = local[0]
        out[block : 2 * block] = values
    longer[2 * block :] = tile.astype(bf16)


def halves_side_by_side(top, bottom, first):
    low = iota(top.shape, 1) < half
    if first:
        return jnp.where(low, top, pltpu.roll(bottom, half, 1))
    return jnp.where(low, pltpu.roll(top, half, 1), bottom)


def rows_again(packed, first):
    turned = pltpu.roll(packed, half, 1)
    return jnp.concatenate([packed, turned] if first else [turned, packed], axis=0)


def sum_parts(parts):
    total = parts[0]
    for k in range(1, parts.shape[0]):
        total = total + parts[k]
    return total


def diagonal_of(place, shape):
    block, width = shape
    return iota(shape, 0) + (place[3] * block - place[4] * width) == iota(shape, 1)


def column_at(place, y_place, z_place):
    return ((place[4] + offsets[y_place]) & 3) + (((place[4] >> 2) + z_place) & 1) * 4


def fill(place, blocks, around, second, right, left, by_col):
    block = left.shape[0]
    base = second * block
    zh, xx, cc = place[0], place[1], place[2]
    ids = [((xx + o) & 3) * 2 + other for other in (cc, 1 - cc) for o in offsets]
    for k, source in enumerate(blocks):
        for z_place, o in enumerate(offsets):
            rows = pl.ds(pl.multiple_of(((zh + o) & 3) * block, block), block)
            right[rows, k * lanes : (k + 1) * lanes] = source[second * 4 + z_place]
    for y_place, source in enumerate(around):
        for z_place in range(2):
            by_col[column_at(place, y_place, z_place)] = source[z_place, base : base + block]
    for k, from_col in enumerate(ids):
        left[:, k * lanes : (k + 1) * lanes] = by_col[from_col]
    return ids


def g_kernel(*refs):
    place, *blocks = refs[:9]
    around = refs[9:13]
    multiplier, segments, ph_segments, lengths, out, more, scale, right, left, by_col = refs[13:]
    block, width = multiplier.shape
    ids = fill(place, blocks, around, 1, right, left, by_col)
    sums = jnp.zeros((extra, lanes), f32)
    for source in around:
        for z_place in range(2):
            sums = sums + source[z_place, 2 * block :].astype(f32)
    blank = jnp.ones((1, lanes - lengths.shape[1]), f32)
    sizes = jnp.concatenate([lengths[...].astype(f32), blank], axis=1)
    mean_d = (sums[0:1] + sums[1:2] + sums[2:3]) / sizes
    mean_u = (sums[3:4] + sums[4:5] + sums[5:6]) / sizes
    shifts = jnp.sum(ph_segments[...] * (2.0 * mean_d), axis=1, keepdims=True)
    scale[...] = jnp.sum(
        segments[...] * (2.0 * (mean_u + penalty * mean_d)), axis=1, keepdims=True
    )
    gram = transposed_dot(left[...], right[...])
    resid = jnp.where(diagonal_of(place, multiplier.shape), shifts, 0.0) - gram
    weight = (multiplier[...].astype(f32) + penalty * resid).astype(bf16)
    term = -2.0 * jnp.dot(weight, right[...], preferred_element_type=f32)
    for k, from_col in enumerate(ids):
        top = term[: block // 2, k * lanes : (k + 1) * lanes]
        bottom = term[block // 2 :, k * lanes : (k + 1) * lanes]
        out[from_col] = halves_side_by_side(top, bottom, True)
        more[from_col] = halves_side_by_side(top, bottom, False)


def q_kernel(*refs):
    place, *blocks = refs[:9]
    around = refs[9:13]
    multiplier, hamiltonian, more, keep, away, right, left, by_col, by_col_out = refs[13:]
    block, width = multiplier.shape
    ids = fill(place, blocks, around, 0, right, left, by_col)
    gram = transposed_dot(left[...], right[...])
    resid = jnp.where(diagonal_of(place, multiplier.shape), shift_value, 0.0) - gram
    weight = (multiplier[...].astype(f32) + penalty * resid).astype(bf16)
    term = -2.0 * jnp.dot(weight, right[...], preferred_element_type=f32)
    energy = 2.0 * jnp.dot(hamiltonian[...], right[...], preferred_element_type=f32)
    term = term + jnp.where((iota(energy.shape, 1) & (lanes - 1)) < half, energy, 0.0)
    for k, from_col in enumerate(ids):
        by_col_out[from_col] = term[:, k * lanes : (k + 1) * lanes]
    for z_place, out in enumerate((keep, away)):
        for y_place in range(4):
            from_col = column_at(place, y_place, z_place)
            out[y_place, :block] = by_col_out[from_col]
            out[y_place, block:] = more[from_col]


def back_kernel(parts, receive_across, back):
    total = rows_again(sum_parts(parts), True)
    back[...] = exact_dot(receive_across[...].astype(f32), total)


def add_kernel(keep, came, *outs):
    for k, out in enumerate(outs):
        out[...] = keep[k] + came[k]


def last_kernel(p0, p1, p2, p3, returned, send, local, scale, density, hole, ph):
    block = local.shape[1]
    total = p0[...] + p1[...] + p2[...] + p3[...]
    ph[...] = rows_again(total[block:], False).T[half:]
    total = total[:block]
    more = exact_dot(send[...].astype(f32), returned[...])
    more = more + 2.0 * scale[...] * local[0].astype(f32)
    total = jnp.where(iota(total.shape, 1) < half, total + more, total).T
    density[...] = total[:half]
    hole[...] = total[half:]


def call(kernel, name, shapes, args, scratch=(), scalars=True, far=(), copies=0, room=8):
    return pl.pallas_call(
        kernel,
        out_shape=[jax.ShapeDtypeStruct(s, d) for s, d in shapes],
        in_specs=[smem] * scalars
        + [hbm if i in far else vmem for i in range(scalars, len(args))],
        out_specs=[vmem] * len(shapes),
        scratch_shapes=[pltpu.VMEM(s, d) for s, d in scratch]
        + [pltpu.SemaphoreType.DMA((copies,))] * (copies > 0),
        compiler_params=pltpu.CompilerParams(vmem_limit_bytes=room * 1024 * 1024),
        name=name,
    )(*args)


def local(
    density_factor,
    hole_factor,
    ph_factor,
    hamiltonian,
    multiplier_q,
    multiplier_g,
    ph_perm,
    block_lengths,
):
    rows, cols = lax.axis_size("row"), lax.axis_size("col")
    block, part = density_factor.shape
    width = multiplier_q.shape[1]
    per = width // block
    padded = rows * group
    place = jnp.stack(
        [digit(axis) for axis in (z_hi, x_axis, core)]
        + [lax.axis_index("row"), lax.axis_index("col")]
    ).astype(i32)
    lengths = block_lengths[None, :]
    perm = ph_perm.reshape(-1, lanes)
    leaving, mine, send, receive, receive_across, segments, ph_segments = call(
        routes_kernel,
        "routes",
        [
            ((padded, lanes), bf16),
            ((2, block, lanes), bf16),
            ((block, padded), bf16),
            ((block, padded), bf16),
            ((padded, block), bf16),
            ((block, lanes), f32),
            ((block, lanes), f32),
        ],
        (place, perm, lengths, density_factor.T, hole_factor.T, ph_factor.T, multiplier_g),
        [((part, block), bf16)] * 3 + [((block, width), bf16)],
        far=(3, 4, 5, 6),
        copies=4,
        room=60,
    )
    incoming = lax.all_to_all(leaving.reshape(rows, group, lanes), "row", 0, 0)
    tall = 2 * block
    body, longer = call(
        rows_kernel,
        "rows",
        [((tall, lanes), bf16), ((tall + extra, lanes), bf16)],
        (incoming.reshape(padded, lanes), receive, mine),
        scalars=False,
    )
    piece = to_column(body, rows, cols, per)
    near = around_digit(piece, z_hi)
    pair_near = jnp.stack([b[:block] for b in near])
    ph_near = jnp.stack([b[block:] for b in near])
    around = gather_cols(longer)
    pair_own = around_ring(pair_near, x_axis, 1)
    ph_own = around_ring(ph_near, x_axis, -1)
    joined = [jnp.concatenate(b) for b in zip(pair_own, ph_own)]
    joined[3], around = lax.optimization_barrier((joined[3], around))
    blocks = joined + [turn(b, core, 1) for b in joined]
    shared = [
        ((width, cols * lanes), bf16),
        ((block, cols * lanes), bf16),
        ((cols, block, lanes), bf16),
    ]
    parts_e, parts_f, scale = call(
        g_kernel,
        "weights_g",
        [((cols, block // 2, lanes), f32), ((cols, block // 2, lanes), f32), ((block, 1), f32)],
        (place, *blocks, *around, multiplier_g, segments, ph_segments, lengths),
        shared,
        room=16,
    )
    long = block + block // 2
    keep, away = call(
        q_kernel,
        "weights_q",
        [((4, long, lanes), f32)] * 2,
        (place, *blocks, *around, multiplier_q, hamiltonian, parts_f),
        shared + [((cols, block, lanes), f32)],
        room=16,
    )
    parts_e, keep, away = lax.optimization_barrier((parts_e, keep, away))
    sums_e = lax.all_to_all(parts_e, "col", 0, 0)
    came = turn(away, z_lo, 1)
    parts = call(add_kernel, "add", [((long, lanes), f32)] * 4, (keep, came), scalars=False)
    sums = [parts[0]] + [turn(p, y_axis, o) for p, o in zip(parts[1:], offsets[1:])]
    (back,) = call(
        back_kernel, "back", [((padded, lanes), f32)], (sums_e, receive_across), scalars=False
    )
    returned = lax.all_to_all(back.reshape(rows, group, lanes), "row", 0, 0)
    grads = call(
        last_kernel,
        "gradients",
        [((part, block), f32)] * 3,
        (*sums, returned.reshape(padded, lanes), send, mine, scale),
        scalars=False,
    )
    return tuple(g.T for g in grads)


def solution(mesh):
    return jax.shard_map(
        local,
        mesh=mesh,
        in_specs=(
            P("row", "col"),
            P("row", "col"),
            P("row", "col"),
            P("row", "col"),
            P("row", "col"),
            P("row", "col"),
            P(),
            P(),
        ),
        out_specs=(P("row", "col"), P("row", "col"), P("row", "col")),
        check_vma=False,
    )
```

```python
import jax
import jax.numpy as jnp
from jax import lax
from jax.experimental import pallas as pl
from jax.experimental.pallas import tpu as pltpu
from jax.sharding import PartitionSpec as P

shift_value = 2.0
penalty = 2.5
both = ("row", "col")
f32 = jnp.float32
bf16 = jnp.bfloat16
i32 = jnp.int32
lanes = 128
half = 64
group = 8
extra = 16
vmem = pl.BlockSpec(memory_space=pltpu.VMEM)
hbm = pl.BlockSpec(memory_space=pltpu.MemorySpace.HBM)
smem = pl.BlockSpec(memory_space=pltpu.SMEM)


z_hi, x_axis, core = ("row", 8, 4), ("row", 2, 4), ("row", 1, 2)
z_lo, y_axis = ("col", 4, 2), ("col", 1, 4)
offsets = (0, -1, 1, 2)


def digit(axis):
    name, stride, length = axis
    return lax.axis_index(name) // stride % length


def turn(x, axis, step):
    name, stride, length = axis
    pairs = []
    for i in range(lax.axis_size(name)):
        d = i // stride % length
        pairs.append((i, i + ((d + step) % length - d) * stride))
    return lax.ppermute(x, name, pairs)


def around_digit(x, axis):
    return [x] + [turn(x, axis, -offset) for offset in offsets[1:]]


def around_ring(x, axis, way):
    near = turn(x, axis, way)
    other = turn(x, axis, -way)
    far = turn(near, axis, way)
    return [x, near, other, far] if way == 1 else [x, other, near, far]


def to_column(x, rows, cols, per):
    pairs = []
    for r in range(rows):
        for c in range(cols):
            pairs.append((r * cols + c, ((r % per) * cols + c) * cols + r // per))
    return lax.ppermute(x, both, pairs)


def iota(shape, axis):
    return lax.broadcasted_iota(i32, shape, axis)


def column_of(row, n):
    return jnp.sum(jnp.where(iota((n, n), 0) == iota((n, n), 1), row, 0), axis=1, keepdims=True)


def row_of(column, n):
    return jnp.sum(jnp.where(iota((n, n), 0) == iota((n, n), 1), column, 0), axis=0, keepdims=True)


def over_block(x):
    return ((x >> 6) * 21846) >> 16


def one_hot(condition, dtype=bf16):
    return jnp.where(condition, 1.0, 0.0).astype(dtype)


def transposed_dot(left, right):
    return lax.dot_general(left, right, (((1,), (1,)), ((), ())), preferred_element_type=f32)


def exact_dot(left, right):
    return jnp.dot(left, right, precision=lax.Precision.HIGHEST, preferred_element_type=f32)


def three_parts(value):
    pieces = []
    for _ in range(3):
        piece = value.astype(bf16).astype(f32)
        pieces.append(piece)
        value = value - piece
    return pieces


def block_of(perm, b, n):
    at = lax.div(b * n, lanes)
    two = jnp.concatenate([perm[pl.ds(at, 1), :], perm[pl.ds(at + 1, 1), :]], axis=1)
    return jnp.where(b * n == at * lanes, two[:, :n], two[:, lanes // 2 : lanes // 2 + n])


def rank_in_block(mine, n):
    column = column_of(mine, n)
    source = over_block(column)
    earlier = (over_block(mine) == source) & (iota((n, n), 1) < iota((n, n), 0))
    return column, source, jnp.sum(jnp.where(earlier, 1, 0), axis=1, keepdims=True)


def routes_kernel(
    place,
    perm,
    lengths,
    density_far,
    hole_far,
    ph_far,
    multiplier_far,
    leaving,
    local,
    send,
    receive,
    receive_across,
    segments,
    ph_segments,
    density,
    hole,
    ph,
    multiplier,
    sems,
):
    fars = (density_far, hole_far, ph_far, multiplier_far)
    copies = [
        pltpu.make_async_copy(far, here, sems.at[i])
        for i, (far, here) in enumerate(zip(fars, (density, hole, ph, multiplier)))
    ]
    for copy in copies:
        copy.start()
    part, block = density.shape
    width = multiplier.shape[1]
    padded = receive_across.shape[0]
    rows = padded // group
    r, c = place[3], place[4]
    square = (block, block)
    ids = r * block + iota((block, 1), 0)
    target = jnp.zeros((block, lanes), i32)
    for g in range(perm.shape[0]):
        target = target + jnp.where(
            perm[g : g + 1, :] == ids, iota((block, lanes), 1) + g * lanes, 0
        )
    target = jnp.sum(target, axis=1, keepdims=True)
    target_row = row_of(target, block)
    spot = jnp.sum(jnp.where(target < target_row, 1, 0), axis=0, keepdims=True)
    spot = spot + (group - block // rows) * over_block(target_row)
    send[...] = one_hot(iota((block, padded), 1) == column_of(spot, block))

    mine_column, source, rank = rank_in_block(block_of(perm, r, block), block)
    slot = source * group + rank
    receive[...] = one_hot(iota((block, padded), 1) == slot)
    receive_across[...] = one_hot(iota((padded, block), 0) == row_of(slot, block))

    for copy in copies:
        copy.wait()
    eye = one_hot(iota(square, 0) == iota(square, 1))
    blank = jnp.zeros((lanes - part, block), bf16)
    pair = transposed_dot(eye, jnp.concatenate([density[...], hole[...]], axis=0))
    tail = transposed_dot(eye, jnp.concatenate([blank, ph[...]], axis=0))
    local[0] = pair.astype(bf16)
    local[1] = tail.astype(bf16)
    gone = transposed_dot(
        one_hot(iota((padded, block), 0) == spot), jnp.concatenate([density[...], blank], axis=0)
    )

    sizes = jnp.concatenate(
        [lengths[...].astype(f32), jnp.zeros((1, lanes - lengths.shape[1]), f32)], axis=1
    )
    upper = one_hot(iota((lanes, lanes), 0) <= iota((lanes, lanes), 1))
    ends = jnp.dot(
        jnp.broadcast_to(sizes, (8, lanes)).astype(bf16), upper, preferred_element_type=f32
    )[0:1]
    starts = ends - sizes
    positions = ids.astype(f32)
    ph_positions = mine_column.astype(f32)
    inside = one_hot((positions >= starts) & (positions < ends), f32)
    ph_inside = one_hot((ph_positions >= starts) & (ph_positions < ends), f32)
    segments[...] = inside
    ph_segments[...] = ph_inside
    first = iota((block, lanes), 1) < half
    density_sq = jnp.sum(jnp.where(first, pair * pair, 0.0), axis=1, keepdims=True)
    on_diag = iota((block, width), 0) + (r * block - c * width) == iota((block, width), 1)
    share = jnp.sum(jnp.where(on_diag, multiplier[...].astype(f32), 0.0), axis=1, keepdims=True)
    share = share - penalty * jnp.sum(tail * tail, axis=1, keepdims=True)
    pieces = three_parts(jnp.sum(inside * density_sq, axis=0, keepdims=True)) + three_parts(
        jnp.sum(ph_inside * share, axis=0, keepdims=True)
    )
    at = iota((padded, lanes), 0) & (group - 1)
    late = iota((padded, lanes), 1) >= half
    for row, piece in enumerate(pieces):
        gone = jnp.where((at == row) & late, pltpu.roll(piece, half, 1), gone)
    leaving[...] = gone.astype(bf16)


def rows_kernel(incoming, receive, local, body, longer):
    block = local.shape[1]
    values = jnp.dot(receive[...], incoming[...], preferred_element_type=f32)
    values = jnp.where(iota(values.shape, 1) < half, values, local[1].astype(f32)).astype(bf16)
    sums = jnp.zeros((group, lanes), f32)
    arrived = incoming[...].astype(f32)
    for g in range(arrived.shape[0] // group):
        sums = sums + arrived[g * group : (g + 1) * group]
    sums = pltpu.roll(sums, half, 1)
    at = iota((extra, lanes), 0)
    tile = jnp.zeros((extra, lanes), f32)
    for k in range(2):
        value = sums[3 * k : 3 * k + 1] + sums[3 * k + 1 : 3 * k + 2] + sums[3 * k + 2 : 3 * k + 3]
        for i, piece in enumerate(three_parts(value)):
            tile = jnp.where(at == 3 * k + i, piece, tile)
    for out in (body, longer):
        out[:block] = local[0]
        out[block : 2 * block] = values
    longer[2 * block :] = tile.astype(bf16)


def halves_side_by_side(top, bottom, first):
    low = iota(top.shape, 1) < half
    if first:
        return jnp.where(low, top, pltpu.roll(bottom, half, 1))
    return jnp.where(low, pltpu.roll(top, half, 1), bottom)


def rows_again(packed, first):
    turned = pltpu.roll(packed, half, 1)
    return jnp.concatenate([packed, turned] if first else [turned, packed], axis=0)


def sum_parts(parts):
    total = parts[0]
    for k in range(1, parts.shape[0]):
        total = total + parts[k]
    return total


def diagonal_of(place, shape):
    block, width = shape
    return iota(shape, 0) + (place[3] * block - place[4] * width) == iota(shape, 1)


def column_at(place, y_place, z_place):
    return ((place[4] + offsets[y_place]) & 3) + (((place[4] >> 2) + z_place) & 1) * 4


def fill(place, blocks, around, second, right, left, by_col):
    block = left.shape[0]
    base = second * block
    zh, xx, cc = place[0], place[1], place[2]
    ids = [((xx + o) & 3) * 2 + other for other in (cc, 1 - cc) for o in offsets]
    for k, source in enumerate(blocks):
        for z_place, o in enumerate(offsets):
            rows = pl.ds(pl.multiple_of(((zh + o) & 3) * block, block), block)
            right[rows, k * lanes : (k + 1) * lanes] = source[second * 4 + z_place]
    for y_place, source in enumerate(around):
        for z_place in range(2):
            by_col[column_at(place, y_place, z_place)] = source[z_place, base : base + block]
    for k, from_col in enumerate(ids):
        left[:, k * lanes : (k + 1) * lanes] = by_col[from_col]
    return ids


def g_kernel(*refs):
    place, *blocks = refs[:9]
    around = refs[9:13]
    multiplier, segments, ph_segments, lengths, out, more, scale, right, left, by_col = refs[13:]
    block, width = multiplier.shape
    ids = fill(place, blocks, around, 1, right, left, by_col)
    sums = jnp.zeros((extra, lanes), f32)
    for source in around:
        for z_place in range(2):
            sums = sums + source[z_place, 2 * block :].astype(f32)
    blank = jnp.ones((1, lanes - lengths.shape[1]), f32)
    sizes = jnp.concatenate([lengths[...].astype(f32), blank], axis=1)
    mean_d = (sums[0:1] + sums[1:2] + sums[2:3]) / sizes
    mean_u = (sums[3:4] + sums[4:5] + sums[5:6]) / sizes
    shifts = jnp.sum(ph_segments[...] * (2.0 * mean_d), axis=1, keepdims=True)
    scale[...] = jnp.sum(
        segments[...] * (2.0 * (mean_u + penalty * mean_d)), axis=1, keepdims=True
    )
    gram = transposed_dot(left[...], right[...])
    resid = jnp.where(diagonal_of(place, multiplier.shape), shifts, 0.0) - gram
    weight = (multiplier[...].astype(f32) + penalty * resid).astype(bf16)
    term = -2.0 * jnp.dot(weight, right[...], preferred_element_type=f32)
    for k, from_col in enumerate(ids):
        top = term[: block // 2, k * lanes : (k + 1) * lanes]
        bottom = term[block // 2 :, k * lanes : (k + 1) * lanes]
        out[from_col] = halves_side_by_side(top, bottom, True)
        more[from_col] = halves_side_by_side(top, bottom, False)


def q_kernel(*refs):
    place, *blocks = refs[:9]
    around = refs[9:13]
    multiplier, hamiltonian, more, keep, away, right, left, by_col, by_col_out = refs[13:]
    block, width = multiplier.shape
    ids = fill(place, blocks, around, 0, right, left, by_col)
    gram = transposed_dot(left[...], right[...])
    resid = jnp.where(diagonal_of(place, multiplier.shape), shift_value, 0.0) - gram
    weight = (multiplier[...].astype(f32) + penalty * resid).astype(bf16)
    term = -2.0 * jnp.dot(weight, right[...], preferred_element_type=f32)
    energy = 2.0 * jnp.dot(hamiltonian[...], right[...], preferred_element_type=f32)
    term = term + jnp.where((iota(energy.shape, 1) & (lanes - 1)) < half, energy, 0.0)
    for k, from_col in enumerate(ids):
        by_col_out[from_col] = term[:, k * lanes : (k + 1) * lanes]
    for z_place, out in enumerate((keep, away)):
        for y_place in range(4):
            from_col = column_at(place, y_place, z_place)
            out[y_place, :block] = by_col_out[from_col]
            out[y_place, block:] = more[from_col]


def back_kernel(parts, receive_across, back):
    total = rows_again(sum_parts(parts), True)
    back[...] = exact_dot(receive_across[...].astype(f32), total)


def add_kernel(keep, came, *outs):
    for k, out in enumerate(outs):
        out[...] = keep[k] + came[k]


def last_kernel(p0, p1, p2, p3, returned, send, local, scale, density, hole, ph):
    block = local.shape[1]
    total = p0[...] + p1[...] + p2[...] + p3[...]
    ph[...] = rows_again(total[block:], False).T[half:]
    total = total[:block]
    more = exact_dot(send[...].astype(f32), returned[...])
    more = more + 2.0 * scale[...] * local[0].astype(f32)
    total = jnp.where(iota(total.shape, 1) < half, total + more, total).T
    density[...] = total[:half]
    hole[...] = total[half:]


def call(kernel, name, shapes, args, scratch=(), scalars=True, far=(), copies=0, room=8):
    return pl.pallas_call(
        kernel,
        out_shape=[jax.ShapeDtypeStruct(s, d) for s, d in shapes],
        in_specs=[smem] * scalars
        + [hbm if i in far else vmem for i in range(scalars, len(args))],
        out_specs=[vmem] * len(shapes),
        scratch_shapes=[pltpu.VMEM(s, d) for s, d in scratch]
        + [pltpu.SemaphoreType.DMA((copies,))] * (copies > 0),
        compiler_params=pltpu.CompilerParams(vmem_limit_bytes=room * 1024 * 1024),
        name=name,
    )(*args)


def local(
    density_factor,
    hole_factor,
    ph_factor,
    hamiltonian,
    multiplier_q,
    multiplier_g,
    ph_perm,
    block_lengths,
):
    rows, cols = lax.axis_size("row"), lax.axis_size("col")
    block, part = density_factor.shape
    width = multiplier_q.shape[1]
    per = width // block
    padded = rows * group
    place = jnp.stack(
        [digit(axis) for axis in (z_hi, x_axis, core)]
        + [lax.axis_index("row"), lax.axis_index("col")]
    ).astype(i32)
    lengths = block_lengths[None, :]
    perm = ph_perm.reshape(-1, lanes)
    leaving, mine, send, receive, receive_across, segments, ph_segments = call(
        routes_kernel,
        "routes",
        [
            ((padded, lanes), bf16),
            ((2, block, lanes), bf16),
            ((block, padded), bf16),
            ((block, padded), bf16),
            ((padded, block), bf16),
            ((block, lanes), f32),
            ((block, lanes), f32),
        ],
        (place, perm, lengths, density_factor.T, hole_factor.T, ph_factor.T, multiplier_g),
        [((part, block), bf16)] * 3 + [((block, width), bf16)],
        far=(3, 4, 5, 6),
        copies=4,
        room=60,
    )
    incoming = lax.all_to_all(leaving.reshape(rows, group, lanes), "row", 0, 0)
    tall = 2 * block
    body, longer = call(
        rows_kernel,
        "rows",
        [((tall, lanes), bf16), ((tall + extra, lanes), bf16)],
        (incoming.reshape(padded, lanes), receive, mine),
        scalars=False,
    )
    piece = to_column(body, rows, cols, per)
    near = around_digit(piece, z_hi)
    pair_near = jnp.stack([b[:block] for b in near])
    ph_near = jnp.stack([b[block:] for b in near])
    two = jnp.stack([longer, turn(longer, z_lo, 1)])
    pair_own = around_ring(pair_near, x_axis, 1)
    ph_own = around_ring(ph_near, x_axis, -1)
    pair_own[1], two = lax.optimization_barrier((pair_own[1], two))
    around = around_digit(two, y_axis)
    joined = [jnp.concatenate(b) for b in zip(pair_own, ph_own)]
    joined[3], around = lax.optimization_barrier((joined[3], around))
    blocks = joined + [turn(b, core, 1) for b in joined]
    shared = [
        ((width, cols * lanes), bf16),
        ((block, cols * lanes), bf16),
        ((cols, block, lanes), bf16),
    ]
    parts_e, parts_f, scale = call(
        g_kernel,
        "weights_g",
        [((cols, block // 2, lanes), f32), ((cols, block // 2, lanes), f32), ((block, 1), f32)],
        (place, *blocks, *around, multiplier_g, segments, ph_segments, lengths),
        shared,
        room=16,
    )
    long = block + block // 2
    keep, away = call(
        q_kernel,
        "weights_q",
        [((4, long, lanes), f32)] * 2,
        (place, *blocks, *around, multiplier_q, hamiltonian, parts_f),
        shared + [((cols, block, lanes), f32)],
        room=16,
    )
    parts_e, keep, away = lax.optimization_barrier((parts_e, keep, away))
    sums_e = lax.all_to_all(parts_e, "col", 0, 0)
    came = turn(away, z_lo, 1)
    parts = call(add_kernel, "add", [((long, lanes), f32)] * 4, (keep, came), scalars=False)
    sums = [parts[0]] + [turn(p, y_axis, o) for p, o in zip(parts[1:], offsets[1:])]
    (back,) = call(
        back_kernel, "back", [((padded, lanes), f32)], (sums_e, receive_across), scalars=False
    )
    returned = lax.all_to_all(back.reshape(rows, group, lanes), "row", 0, 0)
    grads = call(
        last_kernel,
        "gradients",
        [((part, block), f32)] * 3,
        (*sums, returned.reshape(padded, lanes), send, mine, scale),
        scalars=False,
    )
    return tuple(g.T for g in grads)


def solution(mesh):
    return jax.shard_map(
        local,
        mesh=mesh,
        in_specs=(
            P("row", "col"),
            P("row", "col"),
            P("row", "col"),
            P("row", "col"),
            P("row", "col"),
            P("row", "col"),
            P(),
            P(),
        ),
        out_specs=(P("row", "col"), P("row", "col"), P("row", "col")),
        check_vma=False,
    )
```

```python
import jax
import jax.numpy as jnp
from jax import lax
from jax.experimental import pallas as pl
from jax.experimental.pallas import tpu as pltpu
from jax.sharding import PartitionSpec as P

shift_value = 2.0
penalty = 2.5
both = ("row", "col")
f32 = jnp.float32
bf16 = jnp.bfloat16
i32 = jnp.int32
lanes = 128
half = 64
group = 8
extra = 16
vmem = pl.BlockSpec(memory_space=pltpu.VMEM)
hbm = pl.BlockSpec(memory_space=pltpu.MemorySpace.HBM)
smem = pl.BlockSpec(memory_space=pltpu.SMEM)


z_hi, x_axis, core = ("row", 8, 4), ("row", 2, 4), ("row", 1, 2)
z_lo, y_axis = ("col", 4, 2), ("col", 1, 4)
offsets = (0, -1, 1, 2)


def digit(axis):
    name, stride, length = axis
    return lax.axis_index(name) // stride % length


def turn(x, axis, step):
    name, stride, length = axis
    pairs = []
    for i in range(lax.axis_size(name)):
        d = i // stride % length
        pairs.append((i, i + ((d + step) % length - d) * stride))
    return lax.ppermute(x, name, pairs)


def around_digit(x, axis):
    return [x] + [turn(x, axis, -offset) for offset in offsets[1:]]


def around_ring(x, axis, way):
    near = turn(x, axis, way)
    other = turn(x, axis, -way)
    far = turn(near, axis, way)
    return [x, near, other, far] if way == 1 else [x, other, near, far]


def to_column(x, rows, cols, per):
    pairs = []
    for r in range(rows):
        for c in range(cols):
            x_here = r // 2 % 4
            x_there = x_here if c % 2 == 0 else 3 - x_here
            pairs.append((r * cols + c, (c // 2 * 8 + x_there * 2 + r % 2) * cols + r // per))
    return lax.ppermute(x, both, pairs)


def iota(shape, axis):
    return lax.broadcasted_iota(i32, shape, axis)


def column_of(row, n):
    return jnp.sum(jnp.where(iota((n, n), 0) == iota((n, n), 1), row, 0), axis=1, keepdims=True)


def row_of(column, n):
    return jnp.sum(jnp.where(iota((n, n), 0) == iota((n, n), 1), column, 0), axis=0, keepdims=True)


def over_block(x):
    return ((x >> 6) * 21846) >> 16


def one_hot(condition, dtype=bf16):
    return jnp.where(condition, 1.0, 0.0).astype(dtype)


def transposed_dot(left, right):
    return lax.dot_general(left, right, (((1,), (1,)), ((), ())), preferred_element_type=f32)


def exact_dot(left, right):
    return jnp.dot(left, right, precision=lax.Precision.HIGHEST, preferred_element_type=f32)


def three_parts(value):
    pieces = []
    for _ in range(3):
        piece = value.astype(bf16).astype(f32)
        pieces.append(piece)
        value = value - piece
    return pieces


def block_of(perm, b, n):
    at = lax.div(b * n, lanes)
    two = jnp.concatenate([perm[pl.ds(at, 1), :], perm[pl.ds(at + 1, 1), :]], axis=1)
    return jnp.where(b * n == at * lanes, two[:, :n], two[:, lanes // 2 : lanes // 2 + n])


def rank_in_block(mine, n):
    column = column_of(mine, n)
    source = over_block(column)
    earlier = (over_block(mine) == source) & (iota((n, n), 1) < iota((n, n), 0))
    return column, source, jnp.sum(jnp.where(earlier, 1, 0), axis=1, keepdims=True)


def routes_kernel(
    place,
    perm,
    lengths,
    density_far,
    hole_far,
    ph_far,
    multiplier_far,
    leaving,
    local,
    send,
    receive,
    receive_across,
    segments,
    ph_segments,
    density,
    hole,
    ph,
    multiplier,
    sems,
):
    fars = (density_far, hole_far, ph_far, multiplier_far)
    copies = [
        pltpu.make_async_copy(far, here, sems.at[i])
        for i, (far, here) in enumerate(zip(fars, (density, hole, ph, multiplier)))
    ]
    for copy in copies:
        copy.start()
    part, block = density.shape
    width = multiplier.shape[1]
    padded = receive_across.shape[0]
    rows = padded // group
    r, c = place[3], place[4]
    square = (block, block)
    ids = r * block + iota((block, 1), 0)
    target = jnp.zeros((block, lanes), i32)
    for g in range(perm.shape[0]):
        target = target + jnp.where(
            perm[g : g + 1, :] == ids, iota((block, lanes), 1) + g * lanes, 0
        )
    target = jnp.sum(target, axis=1, keepdims=True)
    target_row = row_of(target, block)
    spot = jnp.sum(jnp.where(target < target_row, 1, 0), axis=0, keepdims=True)
    spot = spot + (group - block // rows) * over_block(target_row)
    send[...] = one_hot(iota((block, padded), 1) == column_of(spot, block))

    mine_column, source, rank = rank_in_block(block_of(perm, r, block), block)
    slot = source * group + rank
    receive[...] = one_hot(iota((block, padded), 1) == slot)
    receive_across[...] = one_hot(iota((padded, block), 0) == row_of(slot, block))

    for copy in copies:
        copy.wait()
    eye = one_hot(iota(square, 0) == iota(square, 1))
    blank = jnp.zeros((lanes - part, block), bf16)
    pair = transposed_dot(eye, jnp.concatenate([density[...], hole[...]], axis=0))
    tail = transposed_dot(eye, jnp.concatenate([blank, ph[...]], axis=0))
    local[0] = pair.astype(bf16)
    local[1] = tail.astype(bf16)
    gone = transposed_dot(
        one_hot(iota((padded, block), 0) == spot), jnp.concatenate([density[...], blank], axis=0)
    )

    sizes = jnp.concatenate(
        [lengths[...].astype(f32), jnp.zeros((1, lanes - lengths.shape[1]), f32)], axis=1
    )
    upper = one_hot(iota((lanes, lanes), 0) <= iota((lanes, lanes), 1))
    ends = jnp.dot(
        jnp.broadcast_to(sizes, (8, lanes)).astype(bf16), upper, preferred_element_type=f32
    )[0:1]
    starts = ends - sizes
    positions = ids.astype(f32)
    ph_positions = mine_column.astype(f32)
    inside = one_hot((positions >= starts) & (positions < ends), f32)
    ph_inside = one_hot((ph_positions >= starts) & (ph_positions < ends), f32)
    segments[...] = inside
    ph_segments[...] = ph_inside
    first = iota((block, lanes), 1) < half
    density_sq = jnp.sum(jnp.where(first, pair * pair, 0.0), axis=1, keepdims=True)
    on_diag = iota((block, width), 0) + (r * block - c * width) == iota((block, width), 1)
    share = jnp.sum(jnp.where(on_diag, multiplier[...].astype(f32), 0.0), axis=1, keepdims=True)
    share = share - penalty * jnp.sum(tail * tail, axis=1, keepdims=True)
    pieces = three_parts(jnp.sum(inside * density_sq, axis=0, keepdims=True)) + three_parts(
        jnp.sum(ph_inside * share, axis=0, keepdims=True)
    )
    at = iota((padded, lanes), 0) & (group - 1)
    late = iota((padded, lanes), 1) >= half
    for row, piece in enumerate(pieces):
        gone = jnp.where((at == row) & late, pltpu.roll(piece, half, 1), gone)
    leaving[...] = gone.astype(bf16)


def rows_kernel(incoming, receive, local, body, longer):
    block = local.shape[1]
    values = jnp.dot(receive[...], incoming[...], preferred_element_type=f32)
    values = jnp.where(iota(values.shape, 1) < half, values, local[1].astype(f32)).astype(bf16)
    sums = jnp.zeros((group, lanes), f32)
    arrived = incoming[...].astype(f32)
    for g in range(arrived.shape[0] // group):
        sums = sums + arrived[g * group : (g + 1) * group]
    sums = pltpu.roll(sums, half, 1)
    at = iota((extra, lanes), 0)
    tile = jnp.zeros((extra, lanes), f32)
    for k in range(2):
        value = sums[3 * k : 3 * k + 1] + sums[3 * k + 1 : 3 * k + 2] + sums[3 * k + 2 : 3 * k + 3]
        for i, piece in enumerate(three_parts(value)):
            tile = jnp.where(at == 3 * k + i, piece, tile)
    for out in (body, longer):
        out[:block] = local[0]
        out[block : 2 * block] = values
    longer[2 * block :] = tile.astype(bf16)


def halves_side_by_side(top, bottom, first):
    low = iota(top.shape, 1) < half
    if first:
        return jnp.where(low, top, pltpu.roll(bottom, half, 1))
    return jnp.where(low, pltpu.roll(top, half, 1), bottom)


def rows_again(packed, first):
    turned = pltpu.roll(packed, half, 1)
    return jnp.concatenate([packed, turned] if first else [turned, packed], axis=0)


def sum_parts(parts):
    total = parts[0]
    for k in range(1, parts.shape[0]):
        total = total + parts[k]
    return total


def diagonal_of(place, shape):
    block, width = shape
    return iota(shape, 0) + (place[3] * block - place[4] * width) == iota(shape, 1)


def column_at(place, y_place, z_place):
    return ((place[4] + offsets[y_place]) & 3) + (((place[4] >> 2) + z_place) & 1) * 4


def fill(place, blocks, around, second, right, left, by_col, apart):
    block = left.shape[0]
    base = second * block
    zh, xx, cc = place[0], place[1], place[2]
    ids = [((zh + o) & 3) * 2 + b for o in offsets for b in range(2)]
    for k, source in enumerate(blocks):
        x = (xx + offsets[k % 4]) & 3
        other = cc if k < 4 else 1 - cc
        mirrored = jnp.where((x >> 1) == (place[4] & 1), 0, 1)
        j = (jnp.where(mirrored == 0, x, 3 - x) & 1) * 2 + other
        rows = pl.ds(pl.multiple_of(j * block, block), block)
        for z_place in range(4):
            apart[z_place * 2 + mirrored, rows, :] = source[second * 4 + z_place]
    for k in range(len(ids)):
        right[:, k * lanes : (k + 1) * lanes] = apart[k]
    for y_place, source in enumerate(around):
        for z_place in range(2):
            by_col[column_at(place, y_place, z_place)] = source[z_place, base : base + block]
    for k, from_col in enumerate(ids):
        left[:, k * lanes : (k + 1) * lanes] = by_col[from_col]
    return ids


def g_kernel(*refs):
    place, *blocks = refs[:9]
    around = refs[9:13]
    multiplier, segments, ph_segments, lengths, out, more, scale, right, left, by_col, apart = refs[13:]
    block, width = multiplier.shape
    ids = fill(place, blocks, around, 1, right, left, by_col, apart)
    sums = jnp.zeros((extra, lanes), f32)
    for source in around:
        for z_place in range(2):
            sums = sums + source[z_place, 2 * block :].astype(f32)
    blank = jnp.ones((1, lanes - lengths.shape[1]), f32)
    sizes = jnp.concatenate([lengths[...].astype(f32), blank], axis=1)
    mean_d = (sums[0:1] + sums[1:2] + sums[2:3]) / sizes
    mean_u = (sums[3:4] + sums[4:5] + sums[5:6]) / sizes
    shifts = jnp.sum(ph_segments[...] * (2.0 * mean_d), axis=1, keepdims=True)
    scale[...] = jnp.sum(
        segments[...] * (2.0 * (mean_u + penalty * mean_d)), axis=1, keepdims=True
    )
    gram = transposed_dot(left[...], right[...])
    resid = jnp.where(diagonal_of(place, multiplier.shape), shifts, 0.0) - gram
    weight = (multiplier[...].astype(f32) + penalty * resid).astype(bf16)
    term = -2.0 * jnp.dot(weight, right[...], preferred_element_type=f32)
    for k, from_col in enumerate(ids):
        top = term[: block // 2, k * lanes : (k + 1) * lanes]
        bottom = term[block // 2 :, k * lanes : (k + 1) * lanes]
        out[from_col] = halves_side_by_side(top, bottom, True)
        more[from_col] = halves_side_by_side(top, bottom, False)


def q_kernel(*refs):
    place, *blocks = refs[:9]
    around = refs[9:13]
    multiplier, hamiltonian, more, keep, away, right, left, by_col, apart, by_col_out = refs[13:]
    block, width = multiplier.shape
    ids = fill(place, blocks, around, 0, right, left, by_col, apart)
    gram = transposed_dot(left[...], right[...])
    resid = jnp.where(diagonal_of(place, multiplier.shape), shift_value, 0.0) - gram
    weight = (multiplier[...].astype(f32) + penalty * resid).astype(bf16)
    term = -2.0 * jnp.dot(weight, right[...], preferred_element_type=f32)
    energy = 2.0 * jnp.dot(hamiltonian[...], right[...], preferred_element_type=f32)
    term = term + jnp.where((iota(energy.shape, 1) & (lanes - 1)) < half, energy, 0.0)
    for k, from_col in enumerate(ids):
        by_col_out[from_col] = term[:, k * lanes : (k + 1) * lanes]
    for z_place, out in enumerate((keep, away)):
        for y_place in range(4):
            from_col = column_at(place, y_place, z_place)
            out[y_place, :block] = by_col_out[from_col]
            out[y_place, block:] = more[from_col]


def back_kernel(parts, receive_across, back):
    total = rows_again(sum_parts(parts), True)
    back[...] = exact_dot(receive_across[...].astype(f32), total)


def add_kernel(keep, came, *outs):
    for k, out in enumerate(outs):
        out[...] = keep[k] + came[k]


def last_kernel(p0, p1, p2, p3, returned, send, local, scale, density, hole, ph):
    block = local.shape[1]
    total = p0[...] + p1[...] + p2[...] + p3[...]
    ph[...] = rows_again(total[block:], False).T[half:]
    total = total[:block]
    more = exact_dot(send[...].astype(f32), returned[...])
    more = more + 2.0 * scale[...] * local[0].astype(f32)
    total = jnp.where(iota(total.shape, 1) < half, total + more, total).T
    density[...] = total[:half]
    hole[...] = total[half:]


def call(kernel, name, shapes, args, scratch=(), scalars=True, far=(), copies=0, room=8):
    return pl.pallas_call(
        kernel,
        out_shape=[jax.ShapeDtypeStruct(s, d) for s, d in shapes],
        in_specs=[smem] * scalars
        + [hbm if i in far else vmem for i in range(scalars, len(args))],
        out_specs=[vmem] * len(shapes),
        scratch_shapes=[pltpu.VMEM(s, d) for s, d in scratch]
        + [pltpu.SemaphoreType.DMA((copies,))] * (copies > 0),
        compiler_params=pltpu.CompilerParams(vmem_limit_bytes=room * 1024 * 1024),
        name=name,
    )(*args)


def local(
    density_factor,
    hole_factor,
    ph_factor,
    hamiltonian,
    multiplier_q,
    multiplier_g,
    ph_perm,
    block_lengths,
):
    rows, cols = lax.axis_size("row"), lax.axis_size("col")
    block, part = density_factor.shape
    width = multiplier_q.shape[1]
    per = width // block
    padded = rows * group
    place = jnp.stack(
        [digit(axis) for axis in (z_hi, x_axis, core)]
        + [lax.axis_index("row"), lax.axis_index("col")]
    ).astype(i32)
    lengths = block_lengths[None, :]
    perm = ph_perm.reshape(-1, lanes)
    leaving, mine, send, receive, receive_across, segments, ph_segments = call(
        routes_kernel,
        "routes",
        [
            ((padded, lanes), bf16),
            ((2, block, lanes), bf16),
            ((block, padded), bf16),
            ((block, padded), bf16),
            ((padded, block), bf16),
            ((block, lanes), f32),
            ((block, lanes), f32),
        ],
        (place, perm, lengths, density_factor.T, hole_factor.T, ph_factor.T, multiplier_g),
        [((part, block), bf16)] * 3 + [((block, width), bf16)],
        far=(3, 4, 5, 6),
        copies=4,
        room=60,
    )
    incoming = lax.all_to_all(leaving.reshape(rows, group, lanes), "row", 0, 0)
    tall = 2 * block
    body, longer = call(
        rows_kernel,
        "rows",
        [((tall, lanes), bf16), ((tall + extra, lanes), bf16)],
        (incoming.reshape(padded, lanes), receive, mine),
        scalars=False,
    )
    piece = to_column(body, rows, cols, per)
    near = around_digit(piece, z_hi)
    pair_near = jnp.stack([b[:block] for b in near])
    ph_near = jnp.stack([b[block:] for b in near])
    two = jnp.stack([longer, turn(longer, z_lo, 1)])
    pair_own = around_ring(pair_near, x_axis, 1)
    ph_own = around_ring(ph_near, x_axis, -1)
    pair_own[1], two = lax.optimization_barrier((pair_own[1], two))
    around = around_digit(two, y_axis)
    joined = [jnp.concatenate(b) for b in zip(pair_own, ph_own)]
    joined[3], around = lax.optimization_barrier((joined[3], around))
    blocks = joined + [turn(b, core, 1) for b in joined]
    shared = [
        ((width, cols * lanes), bf16),
        ((block, cols * lanes), bf16),
        ((cols, block, lanes), bf16),
        ((cols, width, lanes), bf16),
    ]
    parts_e, parts_f, scale = call(
        g_kernel,
        "weights_g",
        [((cols, block // 2, lanes), f32), ((cols, block // 2, lanes), f32), ((block, 1), f32)],
        (place, *blocks, *around, multiplier_g, segments, ph_segments, lengths),
        shared,
        room=16,
    )
    long = block + block // 2
    keep, away = call(
        q_kernel,
        "weights_q",
        [((4, long, lanes), f32)] * 2,
        (place, *blocks, *around, multiplier_q, hamiltonian, parts_f),
        shared + [((cols, block, lanes), f32)],
        room=16,
    )
    parts_e, keep, away = lax.optimization_barrier((parts_e, keep, away))
    sums_e = lax.all_to_all(parts_e, "col", 0, 0)
    came = turn(away, z_lo, 1)
    parts = call(add_kernel, "add", [((long, lanes), f32)] * 4, (keep, came), scalars=False)
    sums = [parts[0]] + [turn(p, y_axis, o) for p, o in zip(parts[1:], offsets[1:])]
    (back,) = call(
        back_kernel, "back", [((padded, lanes), f32)], (sums_e, receive_across), scalars=False
    )
    returned = lax.all_to_all(back.reshape(rows, group, lanes), "row", 0, 0)
    grads = call(
        last_kernel,
        "gradients",
        [((part, block), f32)] * 3,
        (*sums, returned.reshape(padded, lanes), send, mine, scale),
        scalars=False,
    )
    return tuple(g.T for g in grads)


def solution(mesh):
    return jax.shard_map(
        local,
        mesh=mesh,
        in_specs=(
            P("row", "col"),
            P("row", "col"),
            P("row", "col"),
            P("row", "col"),
            P("row", "col"),
            P("row", "col"),
            P(),
            P(),
        ),
        out_specs=(P("row", "col"), P("row", "col"), P("row", "col")),
        check_vma=False,
    )
```

```python
import jax
import jax.numpy as jnp
from jax import lax
from jax.experimental import pallas as pl
from jax.experimental.pallas import tpu as pltpu
from jax.sharding import PartitionSpec as P

shift_value = 2.0
penalty = 2.5
both = ("row", "col")
f32 = jnp.float32
bf16 = jnp.bfloat16
i32 = jnp.int32
lanes = 128
half = 64
group = 8
extra = 16
vmem = pl.BlockSpec(memory_space=pltpu.VMEM)
hbm = pl.BlockSpec(memory_space=pltpu.MemorySpace.HBM)
smem = pl.BlockSpec(memory_space=pltpu.SMEM)


z_hi, x_axis, core = ("row", 8, 4), ("row", 2, 4), ("row", 1, 2)
z_lo, y_axis = ("col", 4, 2), ("col", 1, 4)
offsets = (0, -1, 1, 2)


def turn(x, axis, step):
    name, stride, length = axis
    pairs = []
    for i in range(lax.axis_size(name)):
        d = i // stride % length
        pairs.append((i, i + ((d + step) % length - d) * stride))
    return lax.ppermute(x, name, pairs)


def around_digit(x, axis):
    return [x] + [turn(x, axis, -offset) for offset in offsets[1:]]


def around_ring(x, axis, way):
    near = turn(x, axis, way)
    other = turn(x, axis, -way)
    far = turn(near, axis, way)
    return [x, near, other, far] if way == 1 else [x, other, near, far]


def to_column(x, rows, cols, per):
    pairs = []
    for r in range(rows):
        for c in range(cols):
            x_here = r // 2 % 4
            x_there = x_here if c % 2 == 0 else 3 - x_here
            pairs.append((r * cols + c, (c // 2 * 8 + x_there * 2 + r % 2) * cols + r // per))
    return lax.ppermute(x, both, pairs)


def iota(shape, axis):
    return lax.broadcasted_iota(i32, shape, axis)


def column_of(row, n):
    return jnp.sum(jnp.where(iota((n, n), 0) == iota((n, n), 1), row, 0), axis=1, keepdims=True)


def row_of(column, n):
    return jnp.sum(jnp.where(iota((n, n), 0) == iota((n, n), 1), column, 0), axis=0, keepdims=True)


def over_block(x):
    return ((x >> 6) * 21846) >> 16


def one_hot(condition, dtype=bf16):
    return jnp.where(condition, 1.0, 0.0).astype(dtype)


def transposed_dot(left, right):
    return lax.dot_general(left, right, (((1,), (1,)), ((), ())), preferred_element_type=f32)


def exact_dot(left, right):
    return jnp.dot(left, right, precision=lax.Precision.HIGHEST, preferred_element_type=f32)


def three_parts(value):
    pieces = []
    for _ in range(3):
        piece = value.astype(bf16).astype(f32)
        pieces.append(piece)
        value = value - piece
    return pieces


def block_of(perm, b, n):
    at = lax.div(b * n, lanes)
    two = jnp.concatenate([perm[pl.ds(at, 1), :], perm[pl.ds(at + 1, 1), :]], axis=1)
    return jnp.where(b * n == at * lanes, two[:, :n], two[:, lanes // 2 : lanes // 2 + n])


def rank_in_block(mine, n):
    column = column_of(mine, n)
    source = over_block(column)
    earlier = (over_block(mine) == source) & (iota((n, n), 1) < iota((n, n), 0))
    return column, source, jnp.sum(jnp.where(earlier, 1, 0), axis=1, keepdims=True)


def routes_kernel(
    place,
    perm,
    lengths,
    density_far,
    hole_far,
    ph_far,
    multiplier_far,
    leaving,
    local,
    send,
    receive,
    receive_across,
    segments,
    ph_segments,
    density,
    hole,
    ph,
    multiplier,
    sems,
):
    fars = (density_far, hole_far, ph_far, multiplier_far)
    copies = [
        pltpu.make_async_copy(far, here, sems.at[i])
        for i, (far, here) in enumerate(zip(fars, (density, hole, ph, multiplier)))
    ]
    for copy in copies:
        copy.start()
    part, block = density.shape
    width = multiplier.shape[1]
    padded = receive_across.shape[0]
    rows = padded // group
    r, c = place[0], place[1]
    square = (block, block)
    ids = r * block + iota((block, 1), 0)
    target = jnp.zeros((block, lanes), i32)
    for g in range(perm.shape[0]):
        target = target + jnp.where(
            perm[g : g + 1, :] == ids, iota((block, lanes), 1) + g * lanes, 0
        )
    target = jnp.sum(target, axis=1, keepdims=True)
    target_row = row_of(target, block)
    spot = jnp.sum(jnp.where(target < target_row, 1, 0), axis=0, keepdims=True)
    spot = spot + (group - block // rows) * over_block(target_row)
    send[...] = one_hot(iota((block, padded), 1) == column_of(spot, block))

    mine_column, source, rank = rank_in_block(block_of(perm, r, block), block)
    slot = source * group + rank
    receive[...] = one_hot(iota((block, padded), 1) == slot)
    receive_across[...] = one_hot(iota((padded, block), 0) == row_of(slot, block))

    for copy in copies:
        copy.wait()
    eye = one_hot(iota(square, 0) == iota(square, 1))
    blank = jnp.zeros((lanes - part, block), bf16)
    pair = transposed_dot(eye, jnp.concatenate([density[...], hole[...]], axis=0))
    tail = transposed_dot(eye, jnp.concatenate([blank, ph[...]], axis=0))
    local[0] = pair.astype(bf16)
    local[1] = tail.astype(bf16)
    gone = transposed_dot(
        one_hot(iota((padded, block), 0) == spot), jnp.concatenate([density[...], blank], axis=0)
    )

    sizes = jnp.concatenate(
        [lengths[...].astype(f32), jnp.zeros((1, lanes - lengths.shape[1]), f32)], axis=1
    )
    upper = one_hot(iota((lanes, lanes), 0) <= iota((lanes, lanes), 1))
    ends = jnp.dot(
        jnp.broadcast_to(sizes, (8, lanes)).astype(bf16), upper, preferred_element_type=f32
    )[0:1]
    starts = ends - sizes
    positions = ids.astype(f32)
    ph_positions = mine_column.astype(f32)
    inside = one_hot((positions >= starts) & (positions < ends), f32)
    ph_inside = one_hot((ph_positions >= starts) & (ph_positions < ends), f32)
    segments[...] = inside
    ph_segments[...] = ph_inside
    first = iota((block, lanes), 1) < half
    density_sq = jnp.sum(jnp.where(first, pair * pair, 0.0), axis=1, keepdims=True)
    on_diag = iota((block, width), 0) + (r * block - c * width) == iota((block, width), 1)
    share = jnp.sum(jnp.where(on_diag, multiplier[...].astype(f32), 0.0), axis=1, keepdims=True)
    share = share - penalty * jnp.sum(tail * tail, axis=1, keepdims=True)
    pieces = three_parts(jnp.sum(inside * density_sq, axis=0, keepdims=True)) + three_parts(
        jnp.sum(ph_inside * share, axis=0, keepdims=True)
    )
    at = iota((padded, lanes), 0) & (group - 1)
    late = iota((padded, lanes), 1) >= half
    for row, piece in enumerate(pieces):
        gone = jnp.where((at == row) & late, pltpu.roll(piece, half, 1), gone)
    leaving[...] = gone.astype(bf16)


def rows_kernel(incoming, receive, local, body, longer):
    block = local.shape[1]
    values = jnp.dot(receive[...], incoming[...], preferred_element_type=f32)
    values = jnp.where(iota(values.shape, 1) < half, values, local[1].astype(f32)).astype(bf16)
    sums = jnp.zeros((group, lanes), f32)
    arrived = incoming[...].astype(f32)
    for g in range(arrived.shape[0] // group):
        sums = sums + arrived[g * group : (g + 1) * group]
    sums = pltpu.roll(sums, half, 1)
    at = iota((extra, lanes), 0)
    tile = jnp.zeros((extra, lanes), f32)
    for k in range(2):
        value = sums[3 * k : 3 * k + 1] + sums[3 * k + 1 : 3 * k + 2] + sums[3 * k + 2 : 3 * k + 3]
        for i, piece in enumerate(three_parts(value)):
            tile = jnp.where(at == 3 * k + i, piece, tile)
    for out in (body, longer):
        out[:block] = local[0]
        out[block : 2 * block] = values
    longer[2 * block :] = tile.astype(bf16)


def halves_side_by_side(top, bottom, first):
    low = iota(top.shape, 1) < half
    if first:
        return jnp.where(low, top, pltpu.roll(bottom, half, 1))
    return jnp.where(low, pltpu.roll(top, half, 1), bottom)


def rows_again(packed, first):
    turned = pltpu.roll(packed, half, 1)
    return jnp.concatenate([packed, turned] if first else [turned, packed], axis=0)


def sum_parts(parts):
    total = parts[0]
    for k in range(1, parts.shape[0]):
        total = total + parts[k]
    return total


def diagonal_of(place, shape):
    block, width = shape
    return iota(shape, 0) + (place[0] * block - place[1] * width) == iota(shape, 1)


def column_at(place, y_place, z_place):
    return ((place[1] + offsets[y_place]) & 3) + (((place[1] >> 2) + z_place) & 1) * 4


def fill(place, blocks, around, second, right, left, by_col, apart):
    block = left.shape[0]
    base = second * block
    zh, xx, cc = place[0] >> 3, (place[0] >> 1) & 3, place[0] & 1
    ids = [((zh + o) & 3) * 2 + b for o in offsets for b in range(2)]
    for k, source in enumerate(blocks):
        x = (xx + offsets[k % 4]) & 3
        other = cc if k < 4 else 1 - cc
        mirrored = jnp.where((x >> 1) == (place[1] & 1), 0, 1)
        j = (jnp.where(mirrored == 0, x, 3 - x) & 1) * 2 + other
        rows = pl.ds(pl.multiple_of(j * block, block), block)
        for z_place in range(4):
            apart[z_place * 2 + mirrored, rows, :] = source[second * 4 + z_place]
    for k in range(len(ids)):
        right[:, k * lanes : (k + 1) * lanes] = apart[k]
    for y_place, source in enumerate(around):
        for z_place in range(2):
            by_col[column_at(place, y_place, z_place)] = source[z_place, base : base + block]
    for k, from_col in enumerate(ids):
        left[:, k * lanes : (k + 1) * lanes] = by_col[from_col]
    return ids


def g_kernel(*refs):
    place, *blocks = refs[:9]
    around = refs[9:13]
    multiplier, segments, ph_segments, lengths, out, more, scale, right, left, by_col, apart = refs[13:]
    block, width = multiplier.shape
    ids = fill(place, blocks, around, 1, right, left, by_col, apart)
    sums = jnp.zeros((extra, lanes), f32)
    for source in around:
        for z_place in range(2):
            sums = sums + source[z_place, 2 * block :].astype(f32)
    blank = jnp.ones((1, lanes - lengths.shape[1]), f32)
    sizes = jnp.concatenate([lengths[...].astype(f32), blank], axis=1)
    mean_d = (sums[0:1] + sums[1:2] + sums[2:3]) / sizes
    mean_u = (sums[3:4] + sums[4:5] + sums[5:6]) / sizes
    shifts = jnp.sum(ph_segments[...] * (2.0 * mean_d), axis=1, keepdims=True)
    scale[...] = jnp.sum(
        segments[...] * (2.0 * (mean_u + penalty * mean_d)), axis=1, keepdims=True
    )
    gram = transposed_dot(left[...], right[...])
    resid = jnp.where(diagonal_of(place, multiplier.shape), shifts, 0.0) - gram
    weight = (multiplier[...].astype(f32) + penalty * resid).astype(bf16)
    term = -2.0 * jnp.dot(weight, right[...], preferred_element_type=f32)
    for k, from_col in enumerate(ids):
        top = term[: block // 2, k * lanes : (k + 1) * lanes]
        bottom = term[block // 2 :, k * lanes : (k + 1) * lanes]
        out[from_col] = halves_side_by_side(top, bottom, True)
        more[from_col] = halves_side_by_side(top, bottom, False)


def q_kernel(*refs):
    place, *blocks = refs[:9]
    around = refs[9:13]
    multiplier, hamiltonian, more, keep, away, right, left, by_col, apart, by_col_out = refs[13:]
    block, width = multiplier.shape
    ids = fill(place, blocks, around, 0, right, left, by_col, apart)
    gram = transposed_dot(left[...], right[...])
    resid = jnp.where(diagonal_of(place, multiplier.shape), shift_value, 0.0) - gram
    weight = (multiplier[...].astype(f32) + penalty * resid).astype(bf16)
    term = -2.0 * jnp.dot(weight, right[...], preferred_element_type=f32)
    energy = 2.0 * jnp.dot(hamiltonian[...], right[...], preferred_element_type=f32)
    term = term + jnp.where((iota(energy.shape, 1) & (lanes - 1)) < half, energy, 0.0)
    for k, from_col in enumerate(ids):
        by_col_out[from_col] = term[:, k * lanes : (k + 1) * lanes]
    for z_place, out in enumerate((keep, away)):
        for y_place in range(4):
            from_col = column_at(place, y_place, z_place)
            out[y_place, :block] = by_col_out[from_col]
            out[y_place, block:] = more[from_col]


def back_kernel(parts, receive_across, back):
    total = rows_again(sum_parts(parts), True)
    back[...] = exact_dot(receive_across[...].astype(f32), total)


def add_kernel(keep, came, *outs):
    for k, out in enumerate(outs):
        out[...] = keep[k] + came[k]


def last_kernel(p0, p1, p2, p3, returned, send, local, scale, density, hole, ph):
    block = local.shape[1]
    total = p0[...] + p1[...] + p2[...] + p3[...]
    ph[...] = rows_again(total[block:], False).T[half:]
    total = total[:block]
    more = exact_dot(send[...].astype(f32), returned[...])
    more = more + 2.0 * scale[...] * local[0].astype(f32)
    total = jnp.where(iota(total.shape, 1) < half, total + more, total).T
    density[...] = total[:half]
    hole[...] = total[half:]


def call(kernel, name, shapes, args, scratch=(), scalars=True, far=(), copies=0, room=8):
    return pl.pallas_call(
        kernel,
        out_shape=[jax.ShapeDtypeStruct(s, d) for s, d in shapes],
        in_specs=[smem] * scalars
        + [hbm if i in far else vmem for i in range(scalars, len(args))],
        out_specs=[vmem] * len(shapes),
        scratch_shapes=[pltpu.VMEM(s, d) for s, d in scratch]
        + [pltpu.SemaphoreType.DMA((copies,))] * (copies > 0),
        compiler_params=pltpu.CompilerParams(vmem_limit_bytes=room * 1024 * 1024),
        name=name,
    )(*args)


def local(
    density_factor,
    hole_factor,
    ph_factor,
    hamiltonian,
    multiplier_q,
    multiplier_g,
    ph_perm,
    block_lengths,
):
    rows, cols = lax.axis_size("row"), lax.axis_size("col")
    block, part = density_factor.shape
    width = multiplier_q.shape[1]
    per = width // block
    padded = rows * group
    place = jnp.stack([lax.axis_index("row"), lax.axis_index("col")]).astype(i32)
    lengths = block_lengths[None, :]
    perm = ph_perm.reshape(-1, lanes)
    leaving, mine, send, receive, receive_across, segments, ph_segments = call(
        routes_kernel,
        "routes",
        [
            ((padded, lanes), bf16),
            ((2, block, lanes), bf16),
            ((block, padded), bf16),
            ((block, padded), bf16),
            ((padded, block), bf16),
            ((block, lanes), f32),
            ((block, lanes), f32),
        ],
        (place, perm, lengths, density_factor.T, hole_factor.T, ph_factor.T, multiplier_g),
        [((part, block), bf16)] * 3 + [((block, width), bf16)],
        far=(3, 4, 5, 6),
        copies=4,
        room=60,
    )
    incoming = lax.all_to_all(leaving.reshape(rows, group, lanes), "row", 0, 0)
    tall = 2 * block
    body, longer = call(
        rows_kernel,
        "rows",
        [((tall, lanes), bf16), ((tall + extra, lanes), bf16)],
        (incoming.reshape(padded, lanes), receive, mine),
        scalars=False,
    )
    piece = to_column(body, rows, cols, per)
    near = around_digit(piece, z_hi)
    pair_near = jnp.stack([b[:block] for b in near])
    ph_near = jnp.stack([b[block:] for b in near])
    two = jnp.stack([longer, turn(longer, z_lo, 1)])
    pair_own = around_ring(pair_near, x_axis, 1)
    ph_own = around_ring(ph_near, x_axis, -1)
    pair_own[1], two = lax.optimization_barrier((pair_own[1], two))
    around = around_digit(two, y_axis)
    joined = [jnp.concatenate(b) for b in zip(pair_own, ph_own)]
    joined[3], around = lax.optimization_barrier((joined[3], around))
    blocks = joined + [turn(b, core, 1) for b in joined]
    shared = [
        ((width, cols * lanes), bf16),
        ((block, cols * lanes), bf16),
        ((cols, block, lanes), bf16),
        ((cols, width, lanes), bf16),
    ]
    parts_e, parts_f, scale = call(
        g_kernel,
        "weights_g",
        [((cols, block // 2, lanes), f32), ((cols, block // 2, lanes), f32), ((block, 1), f32)],
        (place, *blocks, *around, multiplier_g, segments, ph_segments, lengths),
        shared,
        room=16,
    )
    long = block + block // 2
    keep, away = call(
        q_kernel,
        "weights_q",
        [((4, long, lanes), f32)] * 2,
        (place, *blocks, *around, multiplier_q, hamiltonian, parts_f),
        shared + [((cols, block, lanes), f32)],
        room=16,
    )
    parts_e, keep, away = lax.optimization_barrier((parts_e, keep, away))
    sums_e = lax.all_to_all(parts_e, "col", 0, 0)
    came = turn(away, z_lo, 1)
    parts = call(add_kernel, "add", [((long, lanes), f32)] * 4, (keep, came), scalars=False)
    sums = [parts[0]] + [turn(p, y_axis, o) for p, o in zip(parts[1:], offsets[1:])]
    (back,) = call(
        back_kernel, "back", [((padded, lanes), f32)], (sums_e, receive_across), scalars=False
    )
    returned = lax.all_to_all(back.reshape(rows, group, lanes), "row", 0, 0)
    grads = call(
        last_kernel,
        "gradients",
        [((part, block), f32)] * 3,
        (*sums, returned.reshape(padded, lanes), send, mine, scale),
        scalars=False,
    )
    return tuple(g.T for g in grads)


def solution(mesh):
    return jax.shard_map(
        local,
        mesh=mesh,
        in_specs=(
            P("row", "col"),
            P("row", "col"),
            P("row", "col"),
            P("row", "col"),
            P("row", "col"),
            P("row", "col"),
            P(),
            P(),
        ),
        out_specs=(P("row", "col"), P("row", "col"), P("row", "col")),
        check_vma=False,
    )
```
